32 devices in a mesh: ctx: 8 (over z, core), wsh: 4 (over y, x).
Axes of the slice: x: 2, y: 2, z: 4, core: 2. Of those that a mesh axis runs over, the one named last changes fastest.
Arguments:
- hidden: bfloat16 [4, 1024, 2048], P('wsh', 'ctx'), may hold values from -6 to 6
- cotangent: bfloat16 [4, 1024, 2048], P('wsh', 'ctx'), may hold values from -6 to 6
- doc_ids: int32 [4, 1024], replicated, may hold values from 0 to 3, never falling along the last dimension, each value on 1 to 512 neighbouring positions
- w_qkv: float32 [2048, 3, 2048], P('ctx', None, 'wsh'), may hold values from -4 to 4
- w_out: float32 [2048, 2048], P('wsh', 'ctx'), may hold values from -2 to 2
- w_gu: float32 [2048, 2, 5632], P('ctx', None, 'wsh'), may hold values from -0.125 to 0.125
- w_down: float32 [5632, 2048], P('wsh', 'ctx'), may hold values from -0.078125 to 0.078125
- norm_vecs: float32 [2048, 6], P('ctx'), may hold values from -2 to 2
- first_qkv: float32 [2048, 3, 2048], P('ctx', None, 'wsh'), may hold values from -192 to 192
- first_out: float32 [2048, 2048], P('wsh', 'ctx'), may hold values from -6 to 6
- first_gu: float32 [2048, 2, 5632], P('ctx', None, 'wsh'), may hold values from -40 to 40
- first_down: float32 [5632, 2048], P('wsh', 'ctx'), may hold values from -64 to 64
- first_vecs: float32 [2048, 6], P('ctx'), may hold values from -128 to 128
- second_qkv: float32 [2048, 3, 2048], P('ctx', None, 'wsh'), may hold values from 10 to 100000
- second_out: float32 [2048, 2048], P('wsh', 'ctx'), may hold values from 1 to 100
- second_gu: float32 [2048, 2, 5632], P('ctx', None, 'wsh'), may hold values from 20 to 2000
- second_down: float32 [5632, 2048], P('wsh', 'ctx'), may hold values from 60 to 6000
- second_vecs: float32 [2048, 6], P('ctx'), may hold values from 10 to 10000
Outputs:
- block_out: bfloat16 [4, 1024, 2048], P('wsh', 'ctx')
- grad_hidden: float32 [4, 1024, 2048], P('wsh', 'ctx')
- grad_qkv: float32 [2048, 3, 2048], P('ctx', None, 'wsh')
- grad_out: float32 [2048, 2048], P('wsh', 'ctx')
- grad_gu: float32 [2048, 2, 5632], P('ctx', None, 'wsh')
- grad_down: float32 [5632, 2048], P('wsh', 'ctx')
- grad_vecs: float32 [2048, 6], P('ctx')
- new_qkv: float32 [2048, 3, 2048], P('ctx', None, 'wsh')
- new_out: float32 [2048, 2048], P('wsh', 'ctx')
- new_gu: float32 [2048, 2, 5632], P('ctx', None, 'wsh')
- new_down: float32 [5632, 2048], P('wsh', 'ctx')
- new_vecs: float32 [2048, 6], P('ctx')
- new_first_qkv: float32 [2048, 3, 2048], P('ctx', None, 'wsh')
- new_first_out: float32 [2048, 2048], P('wsh', 'ctx')
- new_first_gu: float32 [2048, 2, 5632], P('ctx', None, 'wsh')
- new_first_down: float32 [5632, 2048], P('wsh', 'ctx')
- new_first_vecs: float32 [2048, 6], P('ctx')
- new_second_qkv: float32 [2048, 3, 2048], P('ctx', None, 'wsh')
- new_second_out: float32 [2048, 2048], P('wsh', 'ctx')
- new_second_gu: float32 [2048, 2, 5632], P('ctx', None, 'wsh')
- new_second_down: float32 [5632, 2048], P('wsh', 'ctx')
- new_second_vecs: float32 [2048, 6], P('ctx')
The draws below stay inside these ranges and needn't reach their ends.
Inputs may be any that keep to these rules, and one draw needn't show every extreme that they name: `doc_ids`: within each sequence the ids never fall, each of the 4 documents holds 1 to 512 positions, and one holds exactly 512.
All inputs are finite; a program needn't handle non-finite values.
Results may differ from the reference program's by a relative error of at most 0.024.
Values may be sent and summed in bfloat16 or wider, within the bound.
No kernel may reach another device: no remote copies, remote signals or barrier semaphores. Data moves between devices by JAX's collectives and lax.ppermute only.
A program may use at most 256 MiB of HBM per device.

```python
import math
import jax
import jax.numpy as jnp
import numpy as np
from jax import lax

D = 2048
H = 32
HD = 64
FF = 5632
ROT = 16
DOCS = 4
STEP = 4
LEN = 1024
SEQS = 4
DOC_MOST = 512


def draw_w_qkv(key, part):
    entries = jnp.clip(jax.random.normal(key, (D, 3, D), jnp.float32), -5.0, 5.0) * D ** (-0.5)
    return entries


def draw_norm_vecs(key, part):
    normal_draw = jnp.clip(jax.random.normal(key, (D, 6), jnp.float32), -4.0, 4.0)
    column_index = jnp.arange(6)
    is_gain = (column_index == 0) | (column_index == 2)
    return jnp.where(is_gain[None, :], 1.0 + 0.2 * normal_draw, 0.3 * normal_draw)


def level_of(stream_key, extent, shards, least, largest):
    def one(position, shards_of):
        draws = jax.random.uniform(jax.random.fold_in(jax.random.fold_in(stream_key, 6), position), (shards_of,), jnp.float32, least / len(shards), largest / len(shards))
        return jnp.repeat(jnp.exp(draws), extent[position] // shards_of).reshape((-1,) + (1,) * (len(extent) - position - 1))

    loudness = one(*shards[0])
    for cut in shards[1:]:
        loudness = loudness * one(*cut)
    return loudness


def split_up(number_of, total, bound, slope):
    portions = [(1 << 20) // math.isqrt(rank ** slope) + 1 for rank in range(2, number_of + 1)]
    surplus, given = total - bound - (number_of - 1), [1] * (number_of - 1)
    while surplus > 0:
        candidates = [i for i in range(number_of - 1) if given[i] < bound]
        pool, remaining = sum([portions[i] for i in candidates]), surplus
        for i in candidates:
            addition = min(bound - given[i], max(1, remaining * portions[i] // pool), surplus)
            given[i] = given[i] + addition
            surplus = surplus - addition
    return np.array([bound] + given)


def ragged_sizes(stream_key, number_of, total, reach, slope):
    if number_of == 2:
        one = jax.random.randint(stream_key, (), max(1, total - reach), min(reach, total - 1) + 1)
        return jnp.stack([one, total - one])
    lengths = jnp.asarray(split_up(number_of, total, reach, slope), jnp.int32)
    twos = (number_of - 1) // 2
    donor, receiver = lengths[1:1 + 2 * twos:2], lengths[2:2 + 2 * twos:2]
    margin = jnp.minimum(donor - 1, reach - receiver)
    moved = jax.random.randint(jax.random.fold_in(stream_key, 1), (twos,), 0, 1 << 20) % (margin + 1)
    lengths = lengths.at[1:1 + 2 * twos:2].set(donor - moved).at[2:2 + 2 * twos:2].set(receiver + moved)
    return lengths[jax.random.permutation(jax.random.fold_in(stream_key, 2), number_of)]


def centred(own_key, shape, width, reach, split=(), held_as=jnp.bfloat16):
    level = level_of(own_key, shape, split, -0.22, 0.18) if split else 1.0
    array = jax.random.normal(own_key, shape, jnp.float32) * width * level
    return jnp.minimum(jnp.maximum(array, -reach), reach).astype(held_as)


def setup_inputs(seed: int = 0) -> dict:
    streams_of = jax.random.split(jax.random.key(seed), 19)
    return {
        "hidden": centred(streams_of[0], (SEQS, LEN, D), 1.0, 6.0, ((0, 4), (1, 8))),
        "cotangent": centred(streams_of[1], (SEQS, LEN, D), 1.0, 6.0, ((0, 4), (1, 8))),
        "doc_ids": jax.vmap(lambda own: jnp.searchsorted(jnp.cumsum(ragged_sizes(own, DOCS, LEN, DOC_MOST, 0)), jnp.arange(LEN), side="right"))(jax.random.split(streams_of[2], SEQS)).reshape((SEQS, LEN)).astype(jnp.int32),
        "w_qkv": draw_w_qkv(jax.random.fold_in(streams_of[18], 71), 0),
        "w_out": centred(streams_of[4], (D, D), (max(D // 256, 1)) ** -0.5, 2.0, ((0, 4), (1, 8)), jnp.float32),
        "w_gu": centred(streams_of[5], (D, 2, FF), D ** -0.5, 0.125, ((0, 8), (2, 4)), jnp.float32),
        "w_down": centred(streams_of[6], (FF, D), FF ** -0.5, 0.078125, ((0, 4), (1, 8)), jnp.float32),
        "norm_vecs": draw_norm_vecs(jax.random.fold_in(streams_of[18], 71), 0),
        "first_qkv": centred(streams_of[8], (D, 3, D), 30.0, 192.0, ((0, 8), (2, 4)), jnp.float32),
        "first_out": centred(streams_of[9], (D, D), 1.5, 6.0, ((0, 4), (1, 8)), jnp.float32),
        "first_gu": centred(streams_of[10], (D, 2, FF), 7.0, 40.0, ((0, 8), (2, 4)), jnp.float32),
        "first_down": centred(streams_of[11], (FF, D), 11.0, 64.0, ((0, 4), (1, 8)), jnp.float32),
        "first_vecs": centred(streams_of[12], (D, 6), 20.0, 128.0, ((0, 8),), jnp.float32),
        "second_qkv": jnp.clip(jnp.exp(math.log(100000.0) - 9.2103404 * jax.random.uniform(streams_of[13], (D, 3, D), jnp.float32) ** level_of(streams_of[13], (D, 3, D), ((0, 8), (2, 4)), -0.2, 0.2)), 10.0, 100000.0),
        "second_out": jnp.clip(jnp.exp(math.log(100.0) - 4.6051702 * jax.random.uniform(streams_of[14], (D, D), jnp.float32) ** level_of(streams_of[14], (D, D), ((0, 4), (1, 8)), -0.2, 0.2)), 1.0, 100.0),
        "second_gu": jnp.clip(jnp.exp(math.log(2000.0) - 4.6051702 * jax.random.uniform(streams_of[15], (D, 2, FF), jnp.float32) ** level_of(streams_of[15], (D, 2, FF), ((0, 8), (2, 4)), -0.2, 0.2)), 20.0, 2000.0),
        "second_down": jnp.clip(jnp.exp(math.log(6000.0) - 4.6051702 * jax.random.uniform(streams_of[16], (FF, D), jnp.float32) ** level_of(streams_of[16], (FF, D), ((0, 4), (1, 8)), -0.2, 0.2)), 60.0, 6000.0),
        "second_vecs": jnp.clip(jnp.exp(math.log(10000.0) - 6.9077553 * jax.random.uniform(streams_of[17], (D, 6), jnp.float32) ** level_of(streams_of[17], (D, 6), ((0, 8),), -0.2, 0.2)), 10.0, 10000.0),
    }


learn_rate = 0.005
beta_first = 0.9
beta_second = 0.95
adam_epsilon = 1e-08
weight_decay = 0.1
norm_epsilon = 1e-05
masked_score = -1e+30

def rounded(matrix):
    return lax.optimization_barrier(matrix.astype(jnp.bfloat16)).astype(jnp.float32)

def layer_norm(matrix, gain_vec, shift_vec):
    centre = matrix - lax.optimization_barrier(jnp.mean(matrix, axis=-1, keepdims=True))
    inverse = lax.rsqrt(lax.optimization_barrier(jnp.mean(centre * centre, axis=-1, keepdims=True)) + norm_epsilon)
    normed = centre * inverse
    return (normed * gain_vec + shift_vec, normed, inverse)

def norm_back(incoming, normed, inverse, gain_vec):
    scaled = incoming * gain_vec
    inner = scaled - lax.optimization_barrier(jnp.mean(scaled, axis=-1, keepdims=True)) - normed * lax.optimization_barrier(jnp.mean(scaled * normed, axis=-1, keepdims=True))
    return (inner * inverse, lax.optimization_barrier(jnp.sum(incoming * normed, axis=0)), lax.optimization_barrier(jnp.sum(incoming, axis=0)))

def rotary_tables(positions):
    half_rot = ROT // 2
    frequency = 10000.0 ** (-2.0 * jnp.arange(half_rot, dtype=jnp.float32) / ROT)
    angles = positions.astype(jnp.float32)[:, None] * frequency[None, :]
    return (jnp.cos(angles), jnp.sin(angles))

def rotate(matrix, cos_table, sin_table, direction):
    per_head = matrix.reshape(matrix.shape[0], matrix.shape[1] // HD, HD)
    half_rot = ROT // 2
    low_part = per_head[:, :, :half_rot]
    high_part = per_head[:, :, half_rot:ROT]
    cos_part = cos_table[:, None, :]
    sin_part = sin_table[:, None, :] * direction
    turned = jnp.concatenate([low_part * cos_part - high_part * sin_part, high_part * cos_part + low_part * sin_part, per_head[:, :, ROT:]], axis=-1)
    return turned.reshape(matrix.shape)

def adam_step(master, gradient, first_moment, second_moment, decay_rate):
    moment_one = beta_first * first_moment + (1.0 - beta_first) * gradient
    moment_two = beta_second * second_moment + (1.0 - beta_second) * gradient * gradient
    corrected = moment_one / (1.0 - beta_first ** STEP)
    spread = jnp.sqrt(moment_two / (1.0 - beta_second ** STEP))
    updated = master - learn_rate * (corrected / (spread + adam_epsilon) + decay_rate * master)
    return (updated, moment_one, moment_two)

def reference(hidden, cotangent, doc_ids, w_qkv, w_out, w_gu, w_down, norm_vecs, first_qkv, first_out, first_gu, first_down, first_vecs, second_qkv, second_out, second_gu, second_down, second_vecs):
    qkv_weight = w_qkv.reshape(D, 3 * D).astype(jnp.bfloat16)
    out_weight = w_out.astype(jnp.bfloat16)
    gu_weight = w_gu.reshape(D, 2 * FF).astype(jnp.bfloat16)
    down_weight = w_down.astype(jnp.bfloat16)
    vectors = rounded(norm_vecs)
    gain_one, shift_one, gain_two, shift_two, bias_query, bias_value = [vectors[:, column] for column in range(6)]
    score_scale = HD ** (-0.5)
    block_rows = min(512, LEN)
    positions = jnp.arange(LEN, dtype=jnp.int32)
    cos_table, sin_table = rotary_tables(positions)
    starts = jnp.arange(LEN // block_rows, dtype=jnp.int32) * block_rows

    def sequence(running, inputs):
        hidden_seq, cot_seq, ids_seq = inputs
        hidden_f32 = hidden_seq.astype(jnp.float32)
        normed_one, hat_one, inverse_one = layer_norm(hidden_f32, gain_one, shift_one)
        normed_one = normed_one.astype(jnp.bfloat16)
        projected = jnp.dot(normed_one, qkv_weight, preferred_element_type=jnp.float32)
        queries = rotate(projected[:, :D] + bias_query, cos_table, sin_table, 1.0).astype(jnp.bfloat16)
        key_rows = rotate(projected[:, D:2 * D], cos_table, sin_table, 1.0).astype(jnp.bfloat16)
        values = (projected[:, 2 * D:] + bias_value).astype(jnp.bfloat16)
        query_f32 = queries.astype(jnp.float32).reshape(LEN, H, HD)
        key_f32 = key_rows.astype(jnp.float32).reshape(LEN, H, HD)
        value_f32 = values.astype(jnp.float32).reshape(LEN, H, HD)

        def visible(row_start):
            query_pos = row_start + jnp.arange(block_rows, dtype=jnp.int32)
            query_ids = lax.dynamic_slice_in_dim(ids_seq, row_start, block_rows, 0)
            return ((positions[None, :] <= query_pos[:, None]) & (ids_seq[None, :] == query_ids[:, None]))[None]

        def scores_of(row_start):
            query_block = lax.dynamic_slice_in_dim(query_f32, row_start, block_rows, 0)
            return (query_block, jnp.einsum('qhd,khd->hqk', query_block, key_f32) * score_scale)

        def forward_block(row_start):
            allowed = visible(row_start)
            query_block, scores = scores_of(row_start)
            row_top = lax.optimization_barrier(jnp.max(jnp.where(allowed, scores, masked_score), axis=-1))
            weights = jnp.where(allowed, jnp.exp(scores - row_top[..., None]), 0.0)
            weight_sum = lax.optimization_barrier(jnp.sum(weights, axis=-1))
            mixed = jnp.einsum('hqk,khd->hqd', rounded(weights), value_f32)
            mixed = (mixed / weight_sum[..., None]).transpose(1, 0, 2).reshape(block_rows, D)
            return (mixed, row_top + jnp.log(weight_sum))
        mixed_blocks, log_blocks = lax.map(forward_block, starts)
        attended = mixed_blocks.reshape(LEN, D).astype(jnp.bfloat16)
        log_sums = log_blocks.transpose(1, 0, 2).reshape(H, LEN)
        middle = hidden_f32 + jnp.dot(attended, out_weight, preferred_element_type=jnp.float32)
        normed_two, hat_two, inverse_two = layer_norm(middle, gain_two, shift_two)
        normed_two = normed_two.astype(jnp.bfloat16)
        gate_up = jnp.dot(normed_two, gu_weight, preferred_element_type=jnp.float32)
        gate_part = gate_up[:, :FF]
        up_part = gate_up[:, FF:]
        sigmoid_gate = jax.nn.sigmoid(gate_part)
        activated = (gate_part * sigmoid_gate * up_part).astype(jnp.bfloat16)
        block_out = (middle + jnp.dot(activated, down_weight, preferred_element_type=jnp.float32)).astype(jnp.bfloat16)
        grad_act = jnp.dot(cot_seq, down_weight.T, preferred_element_type=jnp.float32)
        grad_down = jnp.dot(activated.T, cot_seq, preferred_element_type=jnp.float32)
        grad_gate = grad_act * up_part * sigmoid_gate * (1.0 + gate_part * (1.0 - sigmoid_gate))
        grad_up = grad_act * gate_part * sigmoid_gate
        grad_gate_up = jnp.concatenate([grad_gate, grad_up], axis=1).astype(jnp.bfloat16)
        grad_gu = jnp.dot(normed_two.T, grad_gate_up, preferred_element_type=jnp.float32)
        grad_normed_two = jnp.dot(grad_gate_up, gu_weight.T, preferred_element_type=jnp.float32)
        grad_middle, grad_gain_two, grad_shift_two = norm_back(grad_normed_two, hat_two, inverse_two, gain_two)
        grad_middle = grad_middle + cot_seq.astype(jnp.float32)
        middle_bf16 = grad_middle.astype(jnp.bfloat16)
        grad_out = jnp.dot(attended.T, middle_bf16, preferred_element_type=jnp.float32)
        grad_att = rounded(jnp.dot(middle_bf16, out_weight.T, preferred_element_type=jnp.float32)).reshape(LEN, H, HD)
        deltas = lax.optimization_barrier(jnp.sum(grad_att * attended.astype(jnp.float32).reshape(LEN, H, HD), axis=-1)).T

        def backward_block(running_grads, row_start):
            grad_keys, grad_values = running_grads
            allowed = visible(row_start)
            query_block, scores = scores_of(row_start)
            grad_block = lax.dynamic_slice_in_dim(grad_att, row_start, block_rows, 0)
            log_block = lax.dynamic_slice_in_dim(log_sums, row_start, block_rows, 1)
            delta_block = lax.dynamic_slice_in_dim(deltas, row_start, block_rows, 1)
            probability = jnp.where(allowed, jnp.exp(scores - log_block[..., None]), 0.0)
            grad_values = grad_values + jnp.einsum('hqk,qhd->khd', rounded(probability), grad_block)
            grad_prob = jnp.einsum('qhd,khd->hqk', grad_block, value_f32)
            grad_score = rounded(probability * (grad_prob - delta_block[..., None]) * score_scale)
            grad_query = jnp.einsum('hqk,khd->qhd', grad_score, key_f32)
            grad_keys = grad_keys + jnp.einsum('hqk,qhd->khd', grad_score, query_block)
            return ((grad_keys, grad_values), grad_query.reshape(block_rows, D))
        zero_heads = jnp.zeros((LEN, H, HD), jnp.float32)
        (grad_keys, grad_values), grad_query = lax.scan(backward_block, (zero_heads, zero_heads), starts)
        grad_query = rotate(grad_query.reshape(LEN, D), cos_table, sin_table, -1.0)
        grad_keys = rotate(grad_keys.reshape(LEN, D), cos_table, sin_table, -1.0)
        grad_values = grad_values.reshape(LEN, D)
        grad_rows = jnp.concatenate([grad_query, grad_keys, grad_values], axis=1).astype(jnp.bfloat16)
        grad_qkv = jnp.dot(normed_one.T, grad_rows, preferred_element_type=jnp.float32)
        grad_normed_one = jnp.dot(grad_rows, qkv_weight.T, preferred_element_type=jnp.float32)
        grad_input, grad_gain_one, grad_shift_one = norm_back(grad_normed_one, hat_one, inverse_one, gain_one)
        grad_input = grad_input + grad_middle
        grad_vecs = jnp.stack([grad_gain_one, grad_shift_one, grad_gain_two, grad_shift_two, lax.optimization_barrier(jnp.sum(grad_query, axis=0)), lax.optimization_barrier(jnp.sum(grad_values, axis=0))], axis=1)
        fresh = (grad_qkv, grad_out, grad_gu, grad_down, grad_vecs)
        running = tuple((total_grad + new_grad for total_grad, new_grad in zip(running, fresh)))
        return (running, (block_out, grad_input))
    start_grads = (jnp.zeros((D, 3 * D), jnp.float32), jnp.zeros((D, D), jnp.float32), jnp.zeros((D, 2 * FF), jnp.float32), jnp.zeros((FF, D), jnp.float32), jnp.zeros((D, 6), jnp.float32))
    grads, (block_out, grad_hidden) = lax.scan(sequence, start_grads, (hidden, cotangent, doc_ids))
    grad_qkv, grad_out, grad_gu, grad_down, grad_vecs = grads
    grad_qkv = grad_qkv.reshape(D, 3, D)
    grad_gu = grad_gu.reshape(D, 2, FF)
    new_qkv, new_first_qkv, new_second_qkv = adam_step(w_qkv, grad_qkv, first_qkv, second_qkv, weight_decay)
    new_out, new_first_out, new_second_out = adam_step(w_out, grad_out, first_out, second_out, weight_decay)
    new_gu, new_first_gu, new_second_gu = adam_step(w_gu, grad_gu, first_gu, second_gu, weight_decay)
    new_down, new_first_down, new_second_down = adam_step(w_down, grad_down, first_down, second_down, weight_decay)
    new_vecs, new_first_vecs, new_second_vecs = adam_step(norm_vecs, grad_vecs, first_vecs, second_vecs, 0.0)
    return (block_out, grad_hidden, grad_qkv, grad_out, grad_gu, grad_down, grad_vecs, new_qkv, new_out, new_gu, new_down, new_vecs, new_first_qkv, new_first_out, new_first_gu, new_first_down, new_first_vecs, new_second_qkv, new_second_out, new_second_gu, new_second_down, new_second_vecs)
```

```python
import functools

import jax
import jax.numpy as jnp
from jax import lax
from jax.experimental import pallas as pl
from jax.experimental.pallas import tpu as pltpu
from jax.sharding import PartitionSpec as P

HD = 64
ROT = 16
STEP = 4


learn_rate = 0.005
beta_first = 0.9
beta_second = 0.95
adam_epsilon = 1e-08
weight_decay = 0.1
norm_epsilon = 1e-05
masked_score = -1e30
score_scale = HD ** (-0.5)
F32 = jnp.float32
BF16 = jnp.bfloat16


def swapped(value, axis, bits):
    count = lax.axis_size(axis)
    return lax.ppermute(value, axis, [(source, source ^ bits) for source in range(count)])


def gather_rows(block, axis):
    count = lax.axis_size(axis)
    return [block] + [swapped(block, axis, bits) for bits in range(1, count)]


def scatter_sum(blocks, axis):
    total = blocks[0].astype(F32)
    for bits in range(1, len(blocks)):
        total = total + swapped(blocks[bits], axis, bits).astype(F32)
    return total


def butterfly(value, axis):
    count = lax.axis_size(axis)
    bits = 1
    while bits < count:
        value = value + swapped(value, axis, bits)
        bits *= 2
    return value


def layer_norm(matrix, gain_vec, shift_vec):
    centre = matrix - jnp.mean(matrix, axis=-1, keepdims=True)
    inverse = lax.rsqrt(jnp.mean(centre * centre, axis=-1, keepdims=True) + norm_epsilon)
    normed = centre * inverse
    return (normed * gain_vec + shift_vec, normed, inverse)


def norm_back(incoming, normed, inverse, gain_vec):
    scaled = incoming * gain_vec
    inner = (
        scaled
        - jnp.mean(scaled, axis=-1, keepdims=True)
        - normed * jnp.mean(scaled * normed, axis=-1, keepdims=True)
    )
    return (inner * inverse, jnp.sum(incoming * normed, axis=0), jnp.sum(incoming, axis=0))


def rotary_tables(positions, width):
    half_rot = ROT // 2
    lane = jnp.arange(width, dtype=jnp.int32) % HD
    frequency = 10000.0 ** (-2.0 * (lane % half_rot).astype(F32) / ROT)
    angles = positions.astype(F32)[:, None] * frequency[None, :]
    turning = (lane < ROT)[None, :]
    low_lane = (lane < half_rot)[None, :]
    cosine = jnp.where(turning, jnp.cos(angles), 1.0)
    sine = jnp.where(turning, jnp.sin(angles), 0.0)
    return cosine, jnp.where(low_lane, -sine, 0.0), jnp.where(low_lane, 0.0, sine)


def turned(value, cosine, from_right, from_left):
    width = value.shape[-1]
    half_rot = ROT // 2
    return (
        value * cosine
        + pltpu.roll(value, width - half_rot, 1) * from_right
        + pltpu.roll(value, half_rot, 1) * from_left
    )


def dot_rows(left_side, right_side):
    return lax.dot_general(
        left_side, right_side, (((0,), (0,)), ((), ())), preferred_element_type=F32
    )


def dot_back(left_side, right_side):
    return lax.dot_general(
        left_side, right_side, (((1,), (1,)), ((), ())), preferred_element_type=F32
    )


def dot(left_side, right_side):
    return jnp.dot(left_side, right_side, preferred_element_type=F32)


def adam_step(master, gradient, first_moment, second_moment, decay_rate):
    moment_one = beta_first * first_moment + (1.0 - beta_first) * gradient
    moment_two = beta_second * second_moment + (1.0 - beta_second) * gradient * gradient
    corrected = moment_one / (1.0 - beta_first**STEP)
    spread = jnp.sqrt(moment_two / (1.0 - beta_second**STEP))
    updated = master - learn_rate * (corrected / (spread + adam_epsilon) + decay_rate * master)
    return (updated, moment_one, moment_two)


def kernel_params(megabytes=48):
    return pltpu.CompilerParams(vmem_limit_bytes=megabytes * 1024 * 1024)


def project_kernel(count, groups, *refs):
    blocks = refs[:count]
    gain, shift, bias_q, bias_v, cosine, from_right, from_left, wq, wk, wv = refs[count : count + 10]
    normed_ref, out_ref = refs[count + 10 :]
    rows, _ = blocks[0].shape
    width = wq.shape[1]

    @pl.when(pl.program_id(0) == 0)
    def _():
        for place in range(count):
            value, _, _ = layer_norm(blocks[place][...].astype(F32), gain[...], shift[...])
            normed_ref[place * rows : (place + 1) * rows, :] = value.astype(BF16)

    for which, weight in enumerate((wq, wk, wv)):
        result = dot(normed_ref[...], weight[...])
        if which == 0:
            result = result + bias_q[...]
        if which == 2:
            result = result + bias_v[...]
        for place in range(count):
            part = result[place * rows : (place + 1) * rows]
            if which < 2:
                part = turned(part, cosine[...], from_right[...], from_left[...])
            out_ref[place, 0, :, which * width : (which + 1) * width] = part.astype(BF16)


def project(blocks, gain, shift, bias_q, bias_v, tables, weights, groups):
    count = len(blocks)
    rows, depth = blocks[0].shape
    head_cols = bias_q.shape[1]
    width = head_cols // groups

    def whole(array):
        return pl.BlockSpec(array.shape, lambda g: (0, 0))

    def column(first):
        return pl.BlockSpec((depth, width), lambda g: (0, first * groups + g))

    operands = [*blocks, gain, shift, bias_q, bias_v, *tables]
    specs = [whole(block) for block in blocks] + [whole(gain), whole(shift)]
    specs += [pl.BlockSpec((1, width), lambda g: (0, g))] * 2
    specs += [whole(table) for table in tables]
    specs += [column(0), column(1), column(2)]
    return pl.pallas_call(
        functools.partial(project_kernel, count, groups),
        grid=(groups,),
        in_specs=specs,
        out_specs=[
            pl.BlockSpec((count * rows, depth), lambda g: (0, 0)),
            pl.BlockSpec((count, 1, rows, 3 * width), lambda g: (0, g, 0, 0)),
        ],
        out_shape=[
            jax.ShapeDtypeStruct((count * rows, depth), BF16),
            jax.ShapeDtypeStruct((count, groups, rows, 3 * width), BF16),
        ],
        compiler_params=kernel_params(),
        cost_estimate=pl.CostEstimate(
            flops=2 * count * rows * depth * 3 * head_cols,
            bytes_accessed=2 * depth * 3 * head_cols + 4 * count * rows * depth,
            transcendentals=0,
        ),
        name="project",
    )(*operands, weights, weights, weights)


def windows(length, most, rows):
    for start in range(0, length, rows):
        first = max(0, (start - (most - 1)) // rows * rows)
        yield start, first, start + rows


def seen(start, first, stop, rows, ids_row, ids_col):
    query_pos = start + lax.broadcasted_iota(jnp.int32, (rows, stop - first), 0)
    key_pos = first + lax.broadcasted_iota(jnp.int32, (rows, stop - first), 1)
    same = ids_row[:, first:stop] == ids_col[start : start + rows, :]
    return (key_pos <= query_pos) & same


def head_mask(width, head):
    lane = lax.broadcasted_iota(jnp.int32, (1, width), 1) // HD
    return jnp.where(lane == head, 1.0, 0.0).astype(F32)


def attend_kernel(count, most, step_rows, me_ref, ids_row_ref, ids_col_ref, *refs):
    pieces = refs[:count]
    att_ref, all_ref, lse_ref = refs[count:]
    rows = pieces[0].shape[0]
    width = pieces[0].shape[1] // 3
    length = count * rows
    me = me_ref[0]
    for bits in range(count):
        place = pl.multiple_of((me ^ bits) * rows, rows)
        all_ref[pl.ds(place, rows), :] = pieces[bits][...]
    ids_row = ids_row_ref[...]
    stat_lane = lax.broadcasted_iota(jnp.int32, (step_rows, 128), 1)
    for start, first, stop in windows(length, most, step_rows):
        allowed = seen(start, first, stop, step_rows, ids_row, ids_col_ref)
        query = all_ref[start : start + step_rows, 0:width]
        key = all_ref[first:stop, width : 2 * width]
        value = all_ref[first:stop, 2 * width : 3 * width]
        stats = jnp.zeros((step_rows, 128), F32)
        total = jnp.zeros((step_rows, width), F32)
        for head in range(width // HD):
            mask = head_mask(width, head).astype(BF16)
            scores = dot_back(query * mask, key) * score_scale
            scores = jnp.where(allowed, scores, masked_score)
            top = jnp.max(scores, axis=-1, keepdims=True)
            weights = jnp.exp(scores - top)
            weight_sum = jnp.sum(weights, axis=-1, keepdims=True)
            total = total + dot(weights.astype(BF16), value * mask) / weight_sum
            stats = jnp.where(stat_lane == head, top + jnp.log(weight_sum), stats)
        att_ref[start : start + step_rows, :] = total.astype(BF16)
        lse_ref[start : start + step_rows, :] = stats


def attend(me, ids_row, ids_col, pieces, most):
    count = len(pieces)
    rows, wide = pieces[0].shape
    width = wide // 3
    length = count * rows
    step_rows = min(256, length)
    vmem = pl.BlockSpec(memory_space=pltpu.VMEM)
    return pl.pallas_call(
        functools.partial(attend_kernel, count, most, step_rows),
        in_specs=[pl.BlockSpec(memory_space=pltpu.SMEM)] + [vmem] * (2 + count),
        out_specs=[vmem] * 3,
        out_shape=[
            jax.ShapeDtypeStruct((length, width), BF16),
            jax.ShapeDtypeStruct((length, wide), BF16),
            jax.ShapeDtypeStruct((length, 128), F32),
        ],
        compiler_params=kernel_params(),
        cost_estimate=pl.CostEstimate(
            flops=4 * length * most * width * 4, bytes_accessed=4 * length * wide, transcendentals=0
        ),
        name="attend",
    )(me, ids_row, ids_col, *pieces)


def attend_back_kernel(
    count, most, step_rows, me_ref, ids_row_ref, ids_col_ref, cos_ref, right_ref, left_ref, *refs
):
    pieces = refs[:count]
    att_ref, all_ref, lse_ref, out_ref, sums_ref, grad_ref, dk_ref, dv_ref = refs[count:]
    rows, width = pieces[0].shape
    length = count * rows
    me = me_ref[0]
    for bits in range(count):
        place = pl.multiple_of((me ^ bits) * rows, rows)
        grad_ref[pl.ds(place, rows), :] = pieces[bits][...]
    dk_ref[...] = jnp.zeros_like(dk_ref)
    dv_ref[...] = jnp.zeros_like(dv_ref)
    ids_row = ids_row_ref[...]
    query_sum = jnp.zeros((1, width), F32)
    for start, first, stop in windows(length, most, step_rows):
        own = slice(start, start + step_rows)
        allowed = seen(start, first, stop, step_rows, ids_row, ids_col_ref)
        query = all_ref[own, 0:width]
        key = all_ref[first:stop, width : 2 * width]
        value = all_ref[first:stop, 2 * width : 3 * width]
        incoming = grad_ref[own, :]
        product = incoming.astype(F32) * att_ref[own, :].astype(F32)
        query_grad = jnp.zeros((step_rows, width), F32)
        key_grad = jnp.zeros((stop - first, width), F32)
        value_grad = jnp.zeros((stop - first, width), F32)
        for head in range(width // HD):
            mask32 = head_mask(width, head)
            mask = mask32.astype(BF16)
            delta = jnp.sum(product * mask32, axis=-1, keepdims=True)
            scores = dot_back(query * mask, key) * score_scale
            probability = jnp.where(
                allowed, jnp.exp(scores - lse_ref[own, head : head + 1]), 0.0
            )
            incoming_head = incoming * mask
            value_grad = value_grad + dot_rows(probability.astype(BF16), incoming_head)
            grad_prob = dot_back(incoming_head, value)
            grad_score = (probability * (grad_prob - delta) * score_scale).astype(BF16)
            query_grad = query_grad + dot(grad_score, key * mask)
            key_grad = key_grad + dot_rows(grad_score, query * mask)
        dk_ref[first:stop, :] += key_grad
        dv_ref[first:stop, :] += value_grad
        query_grad = turned(query_grad, cos_ref[own, :], -right_ref[own, :], -left_ref[own, :])
        query_sum = query_sum + jnp.sum(query_grad, axis=0, keepdims=True)
        out_ref[own, 0:width] = query_grad.astype(BF16)
    out_ref[:, width : 2 * width] = turned(
        dk_ref[...], cos_ref[...], -right_ref[...], -left_ref[...]
    ).astype(BF16)
    value_grad = dv_ref[...]
    out_ref[:, 2 * width : 3 * width] = value_grad.astype(BF16)
    value_sum = jnp.sum(value_grad, axis=0, keepdims=True)
    sums_ref[...] = jnp.concatenate(
        [query_sum, value_sum, jnp.zeros((6, width), F32)], axis=0
    )


def attend_back(me, ids_row, ids_col, tables, pieces, att, everything, lse, most):
    count = len(pieces)
    rows, width = pieces[0].shape
    length = count * rows
    step_rows = min(256, length)
    vmem = pl.BlockSpec(memory_space=pltpu.VMEM)
    return pl.pallas_call(
        functools.partial(attend_back_kernel, count, most, step_rows),
        in_specs=[pl.BlockSpec(memory_space=pltpu.SMEM)] + [vmem] * (8 + count),
        out_specs=[vmem] * 2,
        out_shape=[
            jax.ShapeDtypeStruct((length, 3 * width), BF16),
            jax.ShapeDtypeStruct((8, width), F32),
        ],
        scratch_shapes=[
            pltpu.VMEM((length, width), BF16),
            pltpu.VMEM((length, width), F32),
            pltpu.VMEM((length, width), F32),
        ],
        compiler_params=kernel_params(),
        cost_estimate=pl.CostEstimate(
            flops=10 * length * most * width * 4,
            bytes_accessed=16 * length * width,
            transcendentals=0,
        ),
        name="attend_back",
    )(me, ids_row, ids_col, *tables, *pieces, att, everything, lse)


def place_kernel(count, groups, parts, me_ref, *refs):
    pieces = refs[:count]
    out_ref = refs[count]
    rows = pieces[0].shape[0]
    width = pieces[0].shape[1] // parts
    for bits in range(count):
        source = me_ref[0] ^ bits
        row = pl.multiple_of(((source // groups) ^ me_ref[1]) * rows, rows)
        for part in range(parts):
            col = pl.multiple_of((part * groups + source % groups) * width, width)
            out_ref[pl.ds(row, rows), pl.ds(col, width)] = pieces[bits][
                :, part * width : (part + 1) * width
            ]


def place(places, pieces, groups, parts):
    count = len(pieces)
    rows, wide = pieces[0].shape
    vmem = pl.BlockSpec(memory_space=pltpu.VMEM)
    return pl.pallas_call(
        functools.partial(place_kernel, count, groups, parts),
        in_specs=[pl.BlockSpec(memory_space=pltpu.SMEM)] + [vmem] * count,
        out_specs=vmem,
        out_shape=jax.ShapeDtypeStruct((count // groups * rows, groups * wide), BF16),
        compiler_params=kernel_params(),
        cost_estimate=pl.CostEstimate(
            flops=0, bytes_accessed=4 * count * rows * wide, transcendentals=0
        ),
        name="place",
    )(places, *pieces)


def local(
    hidden,
    cotangent,
    doc_ids,
    w_qkv,
    w_out,
    w_gu,
    w_down,
    norm_vecs,
    first_qkv,
    first_out,
    first_gu,
    first_down,
    first_vecs,
    second_qkv,
    second_out,
    second_gu,
    second_down,
    second_vecs,
):
    ctx_size = lax.axis_size("ctx")
    ctx_place = lax.axis_index("ctx")
    shard_count = lax.axis_size("wsh")
    shard_place = lax.axis_index("wsh")
    tok_rows = hidden.shape[1]
    depth = hidden.shape[2]
    length = doc_ids.shape[1]
    most = length // 2
    head_cols = w_qkv.shape[2]
    unit_cols = w_gu.shape[2]
    own_rows = w_qkv.shape[0]
    groups = ctx_size // shard_count
    width = head_cols // groups
    ctx_scalar = ctx_place.astype(jnp.int32).reshape(1)
    places = jnp.stack([ctx_place, shard_place]).astype(jnp.int32)

    vec_cols = jnp.pad(norm_vecs.astype(BF16), ((0, 0), (0, 128 - norm_vecs.shape[1])))
    first_weights = jnp.concatenate(
        [w_qkv.astype(BF16).reshape(own_rows, 3 * head_cols), w_out.astype(BF16).T, vec_cols], axis=1
    )
    first_all = lax.all_gather(first_weights, "ctx", axis=0, tiled=True)
    gu_flat = lax.all_gather(
        w_gu.astype(BF16).reshape(own_rows, 2 * unit_cols), "ctx", axis=0, tiled=True
    )
    down_weight = lax.all_gather(w_down.astype(BF16), "ctx", axis=1, tiled=True)

    hidden_blocks = gather_rows(hidden[0], "wsh")
    cot_all = jnp.concatenate(gather_rows(cotangent[0], "wsh"), axis=0)

    own_seq = ctx_place // groups
    ids_own = lax.dynamic_slice_in_dim(doc_ids, own_seq, 1, 0)
    ids_col = ids_own.reshape(length, 1)
    positions = ctx_place * tok_rows + jnp.arange(tok_rows, dtype=jnp.int32)
    tables = rotary_tables(positions, width)
    tables_all = rotary_tables(jnp.arange(length, dtype=jnp.int32), width)

    vectors = first_all[:, 4 * head_cols : 4 * head_cols + 8].astype(F32).T
    gain_one, shift_one, gain_two, shift_two = [vectors[row : row + 1] for row in range(4)]
    col_start = shard_place * head_cols
    bias_query = lax.dynamic_slice_in_dim(vectors[4:5], col_start, head_cols, 1)
    bias_value = lax.dynamic_slice_in_dim(vectors[5:6], col_start, head_cols, 1)
    qkv_flat = first_all[:, : 3 * head_cols]
    out_turned = first_all[:, 3 * head_cols : 4 * head_cols]

    gathered_one, projected = project(
        hidden_blocks, gain_one, shift_one, bias_query, bias_value, tables, first_all, groups
    )

    def exchange_out(array, bits):
        target = ctx_place ^ bits
        picked = lax.dynamic_slice(
            array,
            ((target // groups) ^ shard_place, target % groups, 0, 0),
            (1, 1) + array.shape[2:],
        )[0, 0]
        return picked if bits == 0 else swapped(picked, "ctx", bits)

    def exchange_back(array, bits):
        picked = lax.dynamic_slice_in_dim(array, (ctx_place ^ bits) * tok_rows, tok_rows, 0)
        return picked if bits == 0 else swapped(picked, "ctx", bits)

    pieces = [exchange_out(projected, bits) for bits in range(ctx_size)]
    att_own, qkv_own, log_sums = attend(ctx_scalar, ids_own, ids_col, pieces, most)
    attended = place(
        places, [exchange_back(att_own, bits) for bits in range(ctx_size)], groups, 1
    )

    def row_blocks(matrix):
        return [
            matrix[place_row * tok_rows : (place_row + 1) * tok_rows]
            for place_row in range(shard_count)
        ]

    attn_terms = dot_back(attended, out_turned).astype(BF16)
    middle = hidden[0].astype(F32) + scatter_sum(row_blocks(attn_terms), "wsh")
    normed_two, hat_two, inverse_two = layer_norm(middle, gain_two, shift_two)
    gathered_two = jnp.concatenate(gather_rows(normed_two.astype(BF16), "wsh"), axis=0)
    gate_up = dot(gathered_two, gu_flat)
    gate_part = gate_up[:, :unit_cols]
    up_part = gate_up[:, unit_cols:]
    sigmoid_gate = jax.nn.sigmoid(gate_part)
    activated = (gate_part * sigmoid_gate * up_part).astype(BF16)
    grad_down = dot_rows(activated, cot_all).astype(BF16)
    share_down = lax.psum_scatter(grad_down, "ctx", scatter_dimension=1, tiled=True).astype(F32)

    grad_act = dot_back(cot_all, down_weight)
    grad_gate = grad_act * up_part * sigmoid_gate * (1.0 + gate_part * (1.0 - sigmoid_gate))
    grad_up = grad_act * gate_part * sigmoid_gate
    grad_gate_up = jnp.concatenate([grad_gate, grad_up], axis=1).astype(BF16)
    grad_gu = dot_rows(gathered_two, grad_gate_up).astype(BF16)
    share_gu = lax.psum_scatter(grad_gu, "ctx", scatter_dimension=0, tiled=True).astype(F32)
    normed_two_terms = dot_back(grad_gate_up, gu_flat).astype(BF16)
    grad_normed_two = scatter_sum(row_blocks(normed_two_terms), "wsh")
    grad_middle, grad_gain_two, grad_shift_two = norm_back(
        grad_normed_two, hat_two, inverse_two, gain_two
    )
    grad_middle = grad_middle + cotangent[0].astype(F32)
    middle_all = jnp.concatenate(gather_rows(grad_middle.astype(BF16), "wsh"), axis=0)
    grad_out = dot_rows(attended, middle_all).astype(BF16)
    share_out = lax.psum_scatter(grad_out, "ctx", scatter_dimension=1, tiled=True).astype(F32)
    grad_att = dot(middle_all, out_turned).astype(BF16)
    grad_att = grad_att.reshape(shard_count, tok_rows, groups, width).transpose(0, 2, 1, 3)
    grad_pieces = [exchange_out(grad_att, bits) for bits in range(ctx_size)]
    grad_own, bias_sums = attend_back(
        ctx_scalar, ids_own, ids_col, tables_all, grad_pieces, att_own, qkv_own, log_sums, most
    )
    grad_rows = place(
        places, [exchange_back(grad_own, bits) for bits in range(ctx_size)], groups, 3
    )
    grad_qkv = dot_rows(gathered_one, grad_rows).astype(BF16)
    share_qkv = lax.psum_scatter(grad_qkv, "ctx", scatter_dimension=0, tiled=True).astype(F32)

    ffn_terms = dot(activated, down_weight).astype(BF16)
    block_out = (middle + scatter_sum(row_blocks(ffn_terms), "wsh")).astype(BF16)

    normed_one_terms = dot_back(grad_rows, qkv_flat).astype(BF16)
    grad_normed_one = scatter_sum(row_blocks(normed_one_terms), "wsh")
    _, hat_one, inverse_one = layer_norm(hidden[0].astype(F32), gain_one, shift_one)
    grad_input, grad_gain_one, grad_shift_one = norm_back(
        grad_normed_one, hat_one, inverse_one, gain_one
    )
    grad_input = grad_input + grad_middle

    bias_start = shard_place * head_cols + (ctx_place % groups) * width
    bias_rows = lax.dynamic_update_slice(
        jnp.zeros((2, depth), F32), bias_sums[:2], (0, bias_start)
    )
    vec_terms = jnp.concatenate(
        [
            grad_gain_one[None],
            grad_shift_one[None],
            grad_gain_two[None],
            grad_shift_two[None],
            bias_rows,
            jnp.zeros((2, depth), F32),
        ],
        axis=0,
    )
    vec_sums = butterfly(butterfly(vec_terms, "ctx"), "wsh")
    share_vecs = lax.dynamic_slice_in_dim(vec_sums, ctx_place * own_rows, own_rows, 1).T[:, :6]

    share_qkv = share_qkv.reshape(w_qkv.shape)
    share_gu = share_gu.reshape(w_gu.shape)
    new_qkv, new_first_qkv, new_second_qkv = adam_step(
        w_qkv, share_qkv, first_qkv, second_qkv, weight_decay
    )
    new_out, new_first_out, new_second_out = adam_step(
        w_out, share_out, first_out, second_out, weight_decay
    )
    new_gu, new_first_gu, new_second_gu = adam_step(
        w_gu, share_gu, first_gu, second_gu, weight_decay
    )
    new_down, new_first_down, new_second_down = adam_step(
        w_down, share_down, first_down, second_down, weight_decay
    )
    new_vecs, new_first_vecs, new_second_vecs = adam_step(
        norm_vecs, share_vecs, first_vecs, second_vecs, 0.0
    )
    return (
        block_out[None],
        grad_input[None],
        share_qkv,
        share_out,
        share_gu,
        share_down,
        share_vecs,
        new_qkv,
        new_out,
        new_gu,
        new_down,
        new_vecs,
        new_first_qkv,
        new_first_out,
        new_first_gu,
        new_first_down,
        new_first_vecs,
        new_second_qkv,
        new_second_out,
        new_second_gu,
        new_second_down,
        new_second_vecs,
    )


def solution(mesh):
    rows = P("wsh", "ctx", None)
    weights = (
        P("ctx", None, "wsh"),
        P("wsh", "ctx"),
        P("ctx", None, "wsh"),
        P("wsh", "ctx"),
        P("ctx", None),
    )
    return jax.shard_map(
        local,
        mesh=mesh,
        in_specs=(rows, rows, P()) + weights * 3,
        out_specs=(rows, rows) + weights * 4,
        check_vma=False,
    )
```

```python
import functools

import jax
import jax.numpy as jnp
from jax import lax
from jax.experimental import pallas as pl
from jax.experimental.pallas import tpu as pltpu
from jax.sharding import PartitionSpec as P


HD = 64
ROT = 16
STEP = 4


learn_rate = 0.005
beta_first = 0.9
beta_second = 0.95
adam_epsilon = 1e-08
weight_decay = 0.1
norm_epsilon = 1e-05
masked_score = -1e30
score_scale = HD ** (-0.5)
F32 = jnp.float32
BF16 = jnp.bfloat16


def swapped(value, axis, bits):
    count = lax.axis_size(axis)
    return lax.ppermute(value, axis, [(source, source ^ bits) for source in range(count)])


def gather_rows(block, axis):
    count = lax.axis_size(axis)
    return [block] + [swapped(block, axis, bits) for bits in range(1, count)]


def scatter_sum(blocks, axis):
    total = blocks[0].astype(F32)
    for bits in range(1, len(blocks)):
        total = total + swapped(blocks[bits], axis, bits).astype(F32)
    return total


def butterfly(value, axis):
    count = lax.axis_size(axis)
    bits = 1
    while bits < count:
        value = value + swapped(value, axis, bits)
        bits *= 2
    return value


def layer_norm(matrix, gain_vec, shift_vec):
    centre = matrix - jnp.mean(matrix, axis=-1, keepdims=True)
    inverse = lax.rsqrt(jnp.mean(centre * centre, axis=-1, keepdims=True) + norm_epsilon)
    normed = centre * inverse
    return (normed * gain_vec + shift_vec, normed, inverse)


def norm_back(incoming, normed, inverse, gain_vec):
    scaled = incoming * gain_vec
    inner = (
        scaled
        - jnp.mean(scaled, axis=-1, keepdims=True)
        - normed * jnp.mean(scaled * normed, axis=-1, keepdims=True)
    )
    return (inner * inverse, jnp.sum(incoming * normed, axis=0), jnp.sum(incoming, axis=0))


def rotary_tables(positions, width):
    half_rot = ROT // 2
    lane = jnp.arange(width, dtype=jnp.int32) % HD
    frequency = 10000.0 ** (-2.0 * (lane % half_rot).astype(F32) / ROT)
    angles = positions.astype(F32)[:, None] * frequency[None, :]
    turning = (lane < ROT)[None, :]
    low_lane = (lane < half_rot)[None, :]
    cosine = jnp.where(turning, jnp.cos(angles), 1.0)
    sine = jnp.where(turning, jnp.sin(angles), 0.0)
    return cosine, jnp.where(low_lane, -sine, 0.0), jnp.where(low_lane, 0.0, sine)


def turned(value, cosine, from_right, from_left):
    width = value.shape[-1]
    half_rot = ROT // 2
    return (
        value * cosine
        + pltpu.roll(value, width - half_rot, 1) * from_right
        + pltpu.roll(value, half_rot, 1) * from_left
    )


def dot_rows(left_side, right_side):
    return lax.dot_general(
        left_side, right_side, (((0,), (0,)), ((), ())), preferred_element_type=F32
    )


def dot_back(left_side, right_side):
    return lax.dot_general(
        left_side, right_side, (((1,), (1,)), ((), ())), preferred_element_type=F32
    )


def dot(left_side, right_side):
    return jnp.dot(left_side, right_side, preferred_element_type=F32)


def adam_step(master, gradient, first_moment, second_moment, decay_rate):
    moment_one = beta_first * first_moment + (1.0 - beta_first) * gradient
    moment_two = beta_second * second_moment + (1.0 - beta_second) * gradient * gradient
    corrected = moment_one / (1.0 - beta_first**STEP)
    spread = jnp.sqrt(moment_two / (1.0 - beta_second**STEP))
    updated = master - learn_rate * (corrected / (spread + adam_epsilon) + decay_rate * master)
    return (updated, moment_one, moment_two)


def kernel_params(megabytes=48):
    return pltpu.CompilerParams(vmem_limit_bytes=megabytes * 1024 * 1024)


def project_kernel(count, *refs):
    blocks = refs[:count]
    gain, shift, bias_q, bias_v, cosine, from_right, from_left, wq, wk, wv = refs[count : count + 10]
    normed_ref, out_ref = refs[count + 10 :]
    rows, _ = blocks[0].shape
    width = wq.shape[1]

    @pl.when(pl.program_id(0) == 0)
    def _():
        for place in range(count):
            value, _, _ = layer_norm(blocks[place][...].astype(F32), gain[...], shift[...])
            normed_ref[place * rows : (place + 1) * rows, :] = value.astype(BF16)

    for which, weight in enumerate((wq, wk, wv)):
        result = dot(normed_ref[...], weight[...])
        if which == 0:
            result = result + bias_q[...]
        if which == 2:
            result = result + bias_v[...]
        for place in range(count):
            part = result[place * rows : (place + 1) * rows]
            if which < 2:
                part = turned(part, cosine[...], from_right[...], from_left[...])
            out_ref[place, 0, :, which * width : (which + 1) * width] = part.astype(BF16)


def project(blocks, gain, shift, bias_q, bias_v, tables, weights, groups):
    count = len(blocks)
    rows, depth = blocks[0].shape
    head_cols = bias_q.shape[1]
    width = head_cols // groups

    def whole(array):
        return pl.BlockSpec(array.shape, lambda g: (0, 0))

    def column(first):
        return pl.BlockSpec((depth, width), lambda g: (0, first * groups + g))

    operands = [*blocks, gain, shift, bias_q, bias_v, *tables]
    specs = [whole(block) for block in blocks] + [whole(gain), whole(shift)]
    specs += [pl.BlockSpec((1, width), lambda g: (0, g))] * 2
    specs += [whole(table) for table in tables]
    specs += [column(0), column(1), column(2)]
    return pl.pallas_call(
        functools.partial(project_kernel, count),
        grid=(groups,),
        in_specs=specs,
        out_specs=[
            pl.BlockSpec((count * rows, depth), lambda g: (0, 0)),
            pl.BlockSpec((count, 1, rows, 3 * width), lambda g: (0, g, 0, 0)),
        ],
        out_shape=[
            jax.ShapeDtypeStruct((count * rows, depth), BF16),
            jax.ShapeDtypeStruct((count, groups, rows, 3 * width), BF16),
        ],
        compiler_params=kernel_params(),
        cost_estimate=pl.CostEstimate(
            flops=2 * count * rows * depth * 3 * head_cols,
            bytes_accessed=2 * depth * 3 * head_cols + 4 * count * rows * depth,
            transcendentals=0,
        ),
        name="project",
    )(*operands, weights, weights, weights)


def windows(length, most, rows):
    for start in range(0, length, rows):
        first = max(0, (start - (most - 1)) // rows * rows)
        yield start, first, start + rows


def seen(start, first, stop, rows, ids_row, ids_col):
    query_pos = start + lax.broadcasted_iota(jnp.int32, (rows, stop - first), 0)
    key_pos = first + lax.broadcasted_iota(jnp.int32, (rows, stop - first), 1)
    same = ids_row[:, first:stop] == ids_col[start : start + rows, :]
    return (key_pos <= query_pos) & same


def head_mask(width, head):
    lane = lax.broadcasted_iota(jnp.int32, (1, width), 1) // HD
    return jnp.where(lane == head, 1.0, 0.0).astype(F32)


def attend_kernel(count, most, step_rows, me_ref, ids_row_ref, ids_col_ref, *refs):
    pieces = refs[:count]
    att_ref, all_ref, lse_ref = refs[count:]
    rows = pieces[0].shape[0]
    width = pieces[0].shape[1] // 3
    length = count * rows
    me = me_ref[0]
    for bits in range(count):
        place = pl.multiple_of((me ^ bits) * rows, rows)
        all_ref[pl.ds(place, rows), :] = pieces[bits][...]
    ids_row = ids_row_ref[...]
    stat_lane = lax.broadcasted_iota(jnp.int32, (step_rows, 128), 1)
    for start, first, stop in windows(length, most, step_rows):
        allowed = seen(start, first, stop, step_rows, ids_row, ids_col_ref)
        query = all_ref[start : start + step_rows, 0:width]
        key = all_ref[first:stop, width : 2 * width]
        value = all_ref[first:stop, 2 * width : 3 * width]
        stats = jnp.zeros((step_rows, 128), F32)
        total = jnp.zeros((step_rows, width), F32)
        for head in range(width // HD):
            mask = head_mask(width, head).astype(BF16)
            scores = dot_back(query * mask, key) * score_scale
            scores = jnp.where(allowed, scores, masked_score)
            top = jnp.max(scores, axis=-1, keepdims=True)
            weights = jnp.exp(scores - top)
            weight_sum = jnp.sum(weights, axis=-1, keepdims=True)
            total = total + dot(weights.astype(BF16), value * mask) / weight_sum
            stats = jnp.where(stat_lane == head, top + jnp.log(weight_sum), stats)
        att_ref[start : start + step_rows, :] = total.astype(BF16)
        lse_ref[start : start + step_rows, :] = stats


def attend(me, ids_row, ids_col, pieces, most):
    count = len(pieces)
    rows, wide = pieces[0].shape
    width = wide // 3
    length = count * rows
    step_rows = min(256, length)
    vmem = pl.BlockSpec(memory_space=pltpu.VMEM)
    return pl.pallas_call(
        functools.partial(attend_kernel, count, most, step_rows),
        in_specs=[pl.BlockSpec(memory_space=pltpu.SMEM)] + [vmem] * (2 + count),
        out_specs=[vmem] * 3,
        out_shape=[
            jax.ShapeDtypeStruct((length, width), BF16),
            jax.ShapeDtypeStruct((length, wide), BF16),
            jax.ShapeDtypeStruct((length, 128), F32),
        ],
        compiler_params=kernel_params(),
        cost_estimate=pl.CostEstimate(
            flops=4 * length * most * width * 4, bytes_accessed=4 * length * wide, transcendentals=0
        ),
        name="attend",
    )(me, ids_row, ids_col, *pieces)


def attend_back_kernel(
    count, most, step_rows, me_ref, ids_row_ref, ids_col_ref, cos_ref, right_ref, left_ref, *refs
):
    pieces = refs[:count]
    att_ref, all_ref, lse_ref, out_ref, sums_ref, grad_ref, dk_ref, dv_ref = refs[count:]
    rows, width = pieces[0].shape
    length = count * rows
    me = me_ref[0]
    for bits in range(count):
        place = pl.multiple_of((me ^ bits) * rows, rows)
        grad_ref[pl.ds(place, rows), :] = pieces[bits][...]
    dk_ref[...] = jnp.zeros_like(dk_ref)
    dv_ref[...] = jnp.zeros_like(dv_ref)
    ids_row = ids_row_ref[...]
    query_sum = jnp.zeros((1, width), F32)
    for start, first, stop in windows(length, most, step_rows):
        own = slice(start, start + step_rows)
        allowed = seen(start, first, stop, step_rows, ids_row, ids_col_ref)
        query = all_ref[own, 0:width]
        key = all_ref[first:stop, width : 2 * width]
        value = all_ref[first:stop, 2 * width : 3 * width]
        incoming = grad_ref[own, :]
        product = incoming.astype(F32) * att_ref[own, :].astype(F32)
        query_grad = jnp.zeros((step_rows, width), F32)
        key_grad = jnp.zeros((stop - first, width), F32)
        value_grad = jnp.zeros((stop - first, width), F32)
        for head in range(width // HD):
            mask32 = head_mask(width, head)
            mask = mask32.astype(BF16)
            delta = jnp.sum(product * mask32, axis=-1, keepdims=True)
            scores = dot_back(query * mask, key) * score_scale
            probability = jnp.where(
                allowed, jnp.exp(scores - lse_ref[own, head : head + 1]), 0.0
            )
            incoming_head = incoming * mask
            value_grad = value_grad + dot_rows(probability.astype(BF16), incoming_head)
            grad_prob = dot_back(incoming_head, value)
            grad_score = (probability * (grad_prob - delta) * score_scale).astype(BF16)
            query_grad = query_grad + dot(grad_score, key * mask)
            key_grad = key_grad + dot_rows(grad_score, query * mask)
        dk_ref[first:stop, :] += key_grad
        dv_ref[first:stop, :] += value_grad
        query_grad = turned(query_grad, cos_ref[own, :], -right_ref[own, :], -left_ref[own, :])
        query_sum = query_sum + jnp.sum(query_grad, axis=0, keepdims=True)
        out_ref[own, 0:width] = query_grad.astype(BF16)
    out_ref[:, width : 2 * width] = turned(
        dk_ref[...], cos_ref[...], -right_ref[...], -left_ref[...]
    ).astype(BF16)
    value_grad = dv_ref[...]
    out_ref[:, 2 * width : 3 * width] = value_grad.astype(BF16)
    value_sum = jnp.sum(value_grad, axis=0, keepdims=True)
    sums_ref[...] = jnp.concatenate(
        [query_sum, value_sum, jnp.zeros((6, width), F32)], axis=0
    )


def attend_back(me, ids_row, ids_col, tables, pieces, att, everything, lse, most):
    count = len(pieces)
    rows, width = pieces[0].shape
    length = count * rows
    step_rows = min(256, length)
    vmem = pl.BlockSpec(memory_space=pltpu.VMEM)
    return pl.pallas_call(
        functools.partial(attend_back_kernel, count, most, step_rows),
        in_specs=[pl.BlockSpec(memory_space=pltpu.SMEM)] + [vmem] * (8 + count),
        out_specs=[vmem] * 2,
        out_shape=[
            jax.ShapeDtypeStruct((length, 3 * width), BF16),
            jax.ShapeDtypeStruct((8, width), F32),
        ],
        scratch_shapes=[
            pltpu.VMEM((length, width), BF16),
            pltpu.VMEM((length, width), F32),
            pltpu.VMEM((length, width), F32),
        ],
        compiler_params=kernel_params(),
        cost_estimate=pl.CostEstimate(
            flops=10 * length * most * width * 4,
            bytes_accessed=16 * length * width,
            transcendentals=0,
        ),
        name="attend_back",
    )(me, ids_row, ids_col, *tables, *pieces, att, everything, lse)


def pack_kernel(qkv_ref, out_ref, vec_ref, packed_ref):
    head_cols = qkv_ref.shape[2]
    for which in range(3):
        packed_ref[:, which * head_cols : (which + 1) * head_cols] = qkv_ref[which].astype(BF16)
    packed_ref[:, 3 * head_cols : 4 * head_cols] = out_ref[...].T.astype(BF16)
    vectors = vec_ref[...]
    padding = jnp.zeros((vectors.shape[0], 128 - vectors.shape[1]), F32)
    packed_ref[:, 4 * head_cols :] = jnp.concatenate([vectors, padding], axis=1).astype(BF16)


def pack(w_qkv, w_out, norm_vecs):
    _, rows, head_cols = w_qkv.shape
    vmem = pl.BlockSpec(memory_space=pltpu.VMEM)
    return pl.pallas_call(
        pack_kernel,
        in_specs=[vmem] * 3,
        out_specs=vmem,
        out_shape=jax.ShapeDtypeStruct((rows, 4 * head_cols + 128), BF16),
        compiler_params=kernel_params(),
        name="pack",
    )(w_qkv, w_out, norm_vecs)


def adam_kernel(leading, share_ref, master_ref, first_ref, second_ref, *outs):
    parts = master_ref.shape[0 if leading else 1]
    cols = master_ref.shape[2]
    for part in range(parts):
        spot = (part,) if leading else (slice(None), part)
        gradient = share_ref[:, part * cols : (part + 1) * cols].astype(F32)
        updates = adam_step(
            master_ref[spot], gradient, first_ref[spot], second_ref[spot], weight_decay
        )
        for out_ref, value in zip(outs, (gradient, *updates)):
            out_ref[spot] = value


def adam_parts(leading, share, *arrays):
    shape = arrays[0].shape
    rows, width = share.shape
    step_rows = max(
        size
        for size in range(16, rows + 1, 16)
        if rows % size == 0 and (size == 16 or size * width <= 100000)
    )
    if leading:
        block = pl.BlockSpec((shape[0], step_rows, shape[2]), lambda step: (0, step, 0))
    else:
        block = pl.BlockSpec((step_rows, shape[1], shape[2]), lambda step: (step, 0, 0))
    return pl.pallas_call(
        functools.partial(adam_kernel, leading),
        grid=(rows // step_rows,),
        in_specs=[pl.BlockSpec((step_rows, width), lambda step: (step, 0))] + [block] * 3,
        out_specs=[block] * 4,
        out_shape=[jax.ShapeDtypeStruct(shape, F32)] * 4,
        compiler_params=kernel_params(),
        cost_estimate=pl.CostEstimate(
            flops=0, bytes_accessed=30 * rows * width, transcendentals=0
        ),
        name="adam",
    )(share, *arrays)


def place_kernel(count, groups, parts, me_ref, *refs):
    pieces = refs[:count]
    out_ref = refs[count]
    rows = pieces[0].shape[0]
    width = pieces[0].shape[1] // parts
    for bits in range(count):
        source = me_ref[0] ^ bits
        row = pl.multiple_of(((source // groups) ^ me_ref[1]) * rows, rows)
        for part in range(parts):
            col = pl.multiple_of((part * groups + source % groups) * width, width)
            out_ref[pl.ds(row, rows), pl.ds(col, width)] = pieces[bits][
                :, part * width : (part + 1) * width
            ]


def place(places, pieces, groups, parts):
    count = len(pieces)
    rows, wide = pieces[0].shape
    vmem = pl.BlockSpec(memory_space=pltpu.VMEM)
    return pl.pallas_call(
        functools.partial(place_kernel, count, groups, parts),
        in_specs=[pl.BlockSpec(memory_space=pltpu.SMEM)] + [vmem] * count,
        out_specs=vmem,
        out_shape=jax.ShapeDtypeStruct((count // groups * rows, groups * wide), BF16),
        compiler_params=kernel_params(),
        cost_estimate=pl.CostEstimate(
            flops=0, bytes_accessed=4 * count * rows * wide, transcendentals=0
        ),
        name="place",
    )(places, *pieces)


def local(
    hidden,
    cotangent,
    doc_ids,
    w_qkv,
    w_out,
    w_gu,
    w_down,
    norm_vecs,
    first_qkv,
    first_out,
    first_gu,
    first_down,
    first_vecs,
    second_qkv,
    second_out,
    second_gu,
    second_down,
    second_vecs,
):
    ctx_size = lax.axis_size("ctx")
    ctx_place = lax.axis_index("ctx")
    shard_count = lax.axis_size("wsh")
    shard_place = lax.axis_index("wsh")
    tok_rows = hidden.shape[1]
    depth = hidden.shape[2]
    length = doc_ids.shape[1]
    most = length // 2
    head_cols = w_qkv.shape[2]
    unit_cols = w_gu.shape[2]
    own_rows = w_qkv.shape[0]
    groups = ctx_size // shard_count
    width = head_cols // groups
    ctx_scalar = ctx_place.astype(jnp.int32).reshape(1)
    places = jnp.stack([ctx_place, shard_place]).astype(jnp.int32)

    first_weights = pack(w_qkv.transpose(1, 0, 2), w_out, norm_vecs)
    first_all = lax.all_gather(first_weights, "ctx", axis=0, tiled=True)
    gu_part = w_gu.astype(BF16).reshape(own_rows, 2 * unit_cols)
    gu_flat = lax.all_gather(gu_part, "ctx", axis=0, tiled=True)
    down_weight = lax.all_gather(w_down.astype(BF16), "ctx", axis=1, tiled=True)

    hidden_blocks = gather_rows(hidden[0], "wsh")
    cot_all = jnp.concatenate(gather_rows(cotangent[0], "wsh"), axis=0)

    own_seq = ctx_place // groups
    ids_own = lax.dynamic_slice_in_dim(doc_ids, own_seq, 1, 0)
    ids_col = ids_own.reshape(length, 1)
    positions = ctx_place * tok_rows + jnp.arange(tok_rows, dtype=jnp.int32)
    tables = rotary_tables(positions, width)
    tables_all = rotary_tables(jnp.arange(length, dtype=jnp.int32), width)

    vectors = first_all[:, 4 * head_cols : 4 * head_cols + 8].astype(F32).T
    gain_one, shift_one, gain_two, shift_two = [vectors[row : row + 1] for row in range(4)]
    col_start = shard_place * head_cols
    bias_query = lax.dynamic_slice_in_dim(vectors[4:5], col_start, head_cols, 1)
    bias_value = lax.dynamic_slice_in_dim(vectors[5:6], col_start, head_cols, 1)
    qkv_flat = first_all[:, : 3 * head_cols]
    out_turned = first_all[:, 3 * head_cols : 4 * head_cols]

    gathered_one, projected = project(
        hidden_blocks, gain_one, shift_one, bias_query, bias_value, tables, first_all, groups
    )

    def exchange_out(array, bits):
        target = ctx_place ^ bits
        picked = lax.dynamic_slice(
            array,
            ((target // groups) ^ shard_place, target % groups, 0, 0),
            (1, 1) + array.shape[2:],
        )[0, 0]
        return picked if bits == 0 else swapped(picked, "ctx", bits)

    def exchange_back(array, bits):
        picked = lax.dynamic_slice_in_dim(array, (ctx_place ^ bits) * tok_rows, tok_rows, 0)
        return picked if bits == 0 else swapped(picked, "ctx", bits)

    pieces = [exchange_out(projected, bits) for bits in range(ctx_size)]
    att_own, qkv_own, log_sums = attend(ctx_scalar, ids_own, ids_col, pieces, most)
    attended = place(
        places, [exchange_back(att_own, bits) for bits in range(ctx_size)], groups, 1
    )

    def row_blocks(matrix):
        return [
            matrix[place_row * tok_rows : (place_row + 1) * tok_rows]
            for place_row in range(shard_count)
        ]

    attn_terms = dot_back(attended, out_turned).astype(BF16)
    middle = hidden[0].astype(F32) + scatter_sum(row_blocks(attn_terms), "wsh")
    normed_two, hat_two, inverse_two = layer_norm(middle, gain_two, shift_two)
    gathered_two = jnp.concatenate(gather_rows(normed_two.astype(BF16), "wsh"), axis=0)
    gate_up = dot(gathered_two, gu_flat)
    gate_part = gate_up[:, :unit_cols]
    activated = (gate_part * jax.nn.sigmoid(gate_part) * gate_up[:, unit_cols:]).astype(BF16)
    grad_down = dot_rows(activated, cot_all).astype(BF16)
    share_down = lax.psum_scatter(grad_down, "ctx", scatter_dimension=1, tiled=True)

    gate_up = lax.optimization_barrier(gate_up)
    gate_part = gate_up[:, :unit_cols]
    up_part = gate_up[:, unit_cols:]
    sigmoid_gate = jax.nn.sigmoid(gate_part)
    grad_act = dot_back(cot_all, down_weight)
    grad_gate = grad_act * up_part * sigmoid_gate * (1.0 + gate_part * (1.0 - sigmoid_gate))
    grad_up = grad_act * gate_part * sigmoid_gate
    grad_gate_up = jnp.concatenate([grad_gate, grad_up], axis=1).astype(BF16)
    grad_gu = dot_rows(gathered_two, grad_gate_up).astype(BF16)
    share_gu = lax.psum_scatter(grad_gu, "ctx", scatter_dimension=0, tiled=True)
    normed_two_terms = dot_back(grad_gate_up, gu_flat).astype(BF16)
    grad_normed_two = scatter_sum(row_blocks(normed_two_terms), "wsh")
    grad_middle, grad_gain_two, grad_shift_two = norm_back(
        grad_normed_two, hat_two, inverse_two, gain_two
    )
    grad_middle = grad_middle + cotangent[0].astype(F32)
    middle_all = jnp.concatenate(gather_rows(grad_middle.astype(BF16), "wsh"), axis=0)
    grad_out = dot_rows(attended, middle_all).astype(BF16)
    share_out = lax.psum_scatter(grad_out, "ctx", scatter_dimension=1, tiled=True)
    grad_att = dot(middle_all, out_turned).astype(BF16)
    grad_att = grad_att.reshape(shard_count, tok_rows, groups, width).transpose(0, 2, 1, 3)
    grad_pieces = [exchange_out(grad_att, bits) for bits in range(ctx_size)]
    grad_own, bias_sums = attend_back(
        ctx_scalar, ids_own, ids_col, tables_all, grad_pieces, att_own, qkv_own, log_sums, most
    )
    grad_rows = place(
        places, [exchange_back(grad_own, bits) for bits in range(ctx_size)], groups, 3
    )
    grad_qkv = dot_rows(gathered_one, grad_rows).astype(BF16)
    share_qkv = lax.psum_scatter(grad_qkv, "ctx", scatter_dimension=0, tiled=True)

    ffn_terms = dot(activated, down_weight).astype(BF16)
    block_out = (middle + scatter_sum(row_blocks(ffn_terms), "wsh")).astype(BF16)

    normed_one_terms = dot_back(grad_rows, qkv_flat).astype(BF16)
    grad_normed_one = scatter_sum(row_blocks(normed_one_terms), "wsh")
    _, hat_one, inverse_one = layer_norm(hidden[0].astype(F32), gain_one, shift_one)
    grad_input, grad_gain_one, grad_shift_one = norm_back(
        grad_normed_one, hat_one, inverse_one, gain_one
    )
    grad_input = grad_input + grad_middle

    bias_start = shard_place * head_cols + (ctx_place % groups) * width
    bias_rows = lax.dynamic_update_slice(
        jnp.zeros((2, depth), F32), bias_sums[:2], (0, bias_start)
    )
    vec_terms = jnp.concatenate(
        [
            grad_gain_one[None],
            grad_shift_one[None],
            grad_gain_two[None],
            grad_shift_two[None],
            bias_rows,
            jnp.zeros((2, depth), F32),
        ],
        axis=0,
    )
    vec_sums = butterfly(butterfly(vec_terms, "ctx"), "wsh")
    share_vecs = lax.dynamic_slice_in_dim(vec_sums, ctx_place * own_rows, own_rows, 1).T[:, :6]

    share_qkv, new_qkv, new_first_qkv, new_second_qkv = [
        array.transpose(1, 0, 2)
        for array in adam_parts(
            True,
            share_qkv,
            *[array.transpose(1, 0, 2) for array in (w_qkv, first_qkv, second_qkv)],
        )
    ]
    share_gu, new_gu, new_first_gu, new_second_gu = adam_parts(
        False, share_gu, w_gu, first_gu, second_gu
    )
    share_down, new_down, new_first_down, new_second_down = [
        array[0]
        for array in adam_parts(True, share_down, w_down[None], first_down[None], second_down[None])
    ]
    share_out, new_out, new_first_out, new_second_out = [
        array[0]
        for array in adam_parts(True, share_out, w_out[None], first_out[None], second_out[None])
    ]
    new_vecs, new_first_vecs, new_second_vecs = adam_step(
        norm_vecs, share_vecs, first_vecs, second_vecs, 0.0
    )
    return (
        block_out[None],
        grad_input[None],
        share_qkv,
        share_out,
        share_gu,
        share_down,
        share_vecs,
        new_qkv,
        new_out,
        new_gu,
        new_down,
        new_vecs,
        new_first_qkv,
        new_first_out,
        new_first_gu,
        new_first_down,
        new_first_vecs,
        new_second_qkv,
        new_second_out,
        new_second_gu,
        new_second_down,
        new_second_vecs,
    )


def solution(mesh):
    rows = P("wsh", "ctx", None)
    weights = (
        P("ctx", None, "wsh"),
        P("wsh", "ctx"),
        P("ctx", None, "wsh"),
        P("wsh", "ctx"),
        P("ctx", None),
    )
    return jax.shard_map(
        local,
        mesh=mesh,
        in_specs=(rows, rows, P()) + weights * 3,
        out_specs=(rows, rows) + weights * 4,
        check_vma=False,
    )
```

```python
import functools

import jax
import jax.numpy as jnp
from jax import lax
from jax.experimental import pallas as pl
from jax.experimental.pallas import tpu as pltpu
from jax.sharding import PartitionSpec as P


HD = 64
ROT = 16
STEP = 4


learn_rate = 0.005
beta_first = 0.9
beta_second = 0.95
adam_epsilon = 1e-08
weight_decay = 0.1
norm_epsilon = 1e-05
masked_score = -1e30
score_scale = HD ** (-0.5)
F32 = jnp.float32
BF16 = jnp.bfloat16


def swapped(value, axis, bits):
    count = lax.axis_size(axis)
    return lax.ppermute(value, axis, [(source, source ^ bits) for source in range(count)])


def gather_rows(block, axis):
    count = lax.axis_size(axis)
    return [block] + [swapped(block, axis, bits) for bits in range(1, count)]


def scatter_sum(blocks, axis):
    total = blocks[0].astype(F32)
    for bits in range(1, len(blocks)):
        total = total + swapped(blocks[bits], axis, bits).astype(F32)
    return total


def butterfly(value, axis):
    count = lax.axis_size(axis)
    bits = 1
    while bits < count:
        value = value + swapped(value, axis, bits)
        bits *= 2
    return value


def chip_scatter(product, halves, axis):
    count = lax.axis_size("ctx")
    own, other = halves
    sent = product(other).astype(BF16)
    total = (product(own) + swapped(sent, "ctx", 1).astype(F32)).astype(BF16)
    return lax.psum_scatter(
        total,
        "ctx",
        scatter_dimension=axis,
        tiled=True,
        axis_index_groups=[list(range(first, count, 2)) for first in range(2)],
    )


def layer_norm(matrix, gain_vec, shift_vec):
    centre = matrix - jnp.mean(matrix, axis=-1, keepdims=True)
    inverse = lax.rsqrt(jnp.mean(centre * centre, axis=-1, keepdims=True) + norm_epsilon)
    normed = centre * inverse
    return (normed * gain_vec + shift_vec, normed, inverse)


def norm_back(incoming, normed, inverse, gain_vec):
    scaled = incoming * gain_vec
    inner = (
        scaled
        - jnp.mean(scaled, axis=-1, keepdims=True)
        - normed * jnp.mean(scaled * normed, axis=-1, keepdims=True)
    )
    return (inner * inverse, jnp.sum(incoming * normed, axis=0), jnp.sum(incoming, axis=0))


def rotary_tables(positions, width):
    half_rot = ROT // 2
    lane = jnp.arange(width, dtype=jnp.int32) % HD
    frequency = 10000.0 ** (-2.0 * (lane % half_rot).astype(F32) / ROT)
    angles = positions.astype(F32)[:, None] * frequency[None, :]
    turning = (lane < ROT)[None, :]
    low_lane = (lane < half_rot)[None, :]
    cosine = jnp.where(turning, jnp.cos(angles), 1.0)
    sine = jnp.where(turning, jnp.sin(angles), 0.0)
    return cosine, jnp.where(low_lane, -sine, 0.0), jnp.where(low_lane, 0.0, sine)


def turned(value, cosine, from_right, from_left):
    width = value.shape[-1]
    half_rot = ROT // 2
    return (
        value * cosine
        + pltpu.roll(value, width - half_rot, 1) * from_right
        + pltpu.roll(value, half_rot, 1) * from_left
    )


def dot_rows(left_side, right_side):
    return lax.dot_general(
        left_side, right_side, (((0,), (0,)), ((), ())), preferred_element_type=F32
    )


def dot_back(left_side, right_side):
    return lax.dot_general(
        left_side, right_side, (((1,), (1,)), ((), ())), preferred_element_type=F32
    )


def dot(left_side, right_side):
    return jnp.dot(left_side, right_side, preferred_element_type=F32)


def adam_step(master, gradient, first_moment, second_moment, decay_rate):
    moment_one = beta_first * first_moment + (1.0 - beta_first) * gradient
    moment_two = beta_second * second_moment + (1.0 - beta_second) * gradient * gradient
    corrected = moment_one / (1.0 - beta_first**STEP)
    spread = jnp.sqrt(moment_two / (1.0 - beta_second**STEP))
    updated = master - learn_rate * (corrected / (spread + adam_epsilon) + decay_rate * master)
    return (updated, moment_one, moment_two)


def kernel_params(megabytes=48):
    return pltpu.CompilerParams(vmem_limit_bytes=megabytes * 1024 * 1024)


def project_kernel(count, *refs):
    blocks = refs[:count]
    gain, shift, bias_q, bias_v, cosine, from_right, from_left, wq, wk, wv = refs[count : count + 10]
    normed_ref, out_ref = refs[count + 10 :]
    rows, _ = blocks[0].shape
    width = wq.shape[1]

    @pl.when(pl.program_id(0) == 0)
    def _():
        for place in range(count):
            value, _, _ = layer_norm(blocks[place][...].astype(F32), gain[...], shift[...])
            normed_ref[place * rows : (place + 1) * rows, :] = value.astype(BF16)

    for which, weight in enumerate((wq, wk, wv)):
        result = dot(normed_ref[...], weight[...])
        if which == 0:
            result = result + bias_q[...]
        if which == 2:
            result = result + bias_v[...]
        for place in range(count):
            part = result[place * rows : (place + 1) * rows]
            if which < 2:
                part = turned(part, cosine[...], from_right[...], from_left[...])
            out_ref[place, 0, :, which * width : (which + 1) * width] = part.astype(BF16)


def project(blocks, gain, shift, bias_q, bias_v, tables, weights, groups):
    count = len(blocks)
    rows, depth = blocks[0].shape
    head_cols = bias_q.shape[1]
    width = head_cols // groups

    def whole(array):
        return pl.BlockSpec(array.shape, lambda g: (0, 0))

    def column(first):
        return pl.BlockSpec((depth, width), lambda g: (0, first * groups + g))

    operands = [*blocks, gain, shift, bias_q, bias_v, *tables]
    specs = [whole(block) for block in blocks] + [whole(gain), whole(shift)]
    specs += [pl.BlockSpec((1, width), lambda g: (0, g))] * 2
    specs += [whole(table) for table in tables]
    specs += [column(0), column(1), column(2)]
    return pl.pallas_call(
        functools.partial(project_kernel, count),
        grid=(groups,),
        in_specs=specs,
        out_specs=[
            pl.BlockSpec((count * rows, depth), lambda g: (0, 0)),
            pl.BlockSpec((count, 1, rows, 3 * width), lambda g: (0, g, 0, 0)),
        ],
        out_shape=[
            jax.ShapeDtypeStruct((count * rows, depth), BF16),
            jax.ShapeDtypeStruct((count, groups, rows, 3 * width), BF16),
        ],
        compiler_params=kernel_params(),
        cost_estimate=pl.CostEstimate(
            flops=2 * count * rows * depth * 3 * head_cols,
            bytes_accessed=2 * depth * 3 * head_cols + 4 * count * rows * depth,
            transcendentals=0,
        ),
        name="project",
    )(*operands, weights, weights, weights)


def windows(length, most, rows):
    for start in range(0, length, rows):
        first = max(0, (start - (most - 1)) // rows * rows)
        yield start, first, start + rows


def seen(start, first, stop, rows, ids_row, ids_col):
    query_pos = start + lax.broadcasted_iota(jnp.int32, (rows, stop - first), 0)
    key_pos = first + lax.broadcasted_iota(jnp.int32, (rows, stop - first), 1)
    same = ids_row[:, first:stop] == ids_col[start : start + rows, :]
    return (key_pos <= query_pos) & same


def head_mask(width, head):
    lane = lax.broadcasted_iota(jnp.int32, (1, width), 1) // HD
    return jnp.where(lane == head, 1.0, 0.0).astype(F32)


def attend_kernel(count, most, step_rows, me_ref, ids_row_ref, ids_col_ref, *refs):
    pieces = refs[:count]
    att_ref, all_ref, lse_ref = refs[count:]
    rows = pieces[0].shape[0]
    width = pieces[0].shape[1] // 3
    length = count * rows
    me = me_ref[0]
    for bits in range(count):
        place = pl.multiple_of((me ^ bits) * rows, rows)
        all_ref[pl.ds(place, rows), :] = pieces[bits][...]
    ids_row = ids_row_ref[...]
    stat_lane = lax.broadcasted_iota(jnp.int32, (step_rows, 128), 1)
    for start, first, stop in windows(length, most, step_rows):
        allowed = seen(start, first, stop, step_rows, ids_row, ids_col_ref)
        query = all_ref[start : start + step_rows, 0:width]
        key = all_ref[first:stop, width : 2 * width]
        value = all_ref[first:stop, 2 * width : 3 * width]
        stats = jnp.zeros((step_rows, 128), F32)
        total = jnp.zeros((step_rows, width), F32)
        for head in range(width // HD):
            mask = head_mask(width, head).astype(BF16)
            scores = dot_back(query * mask, key) * score_scale
            scores = jnp.where(allowed, scores, masked_score)
            top = jnp.max(scores, axis=-1, keepdims=True)
            weights = jnp.exp(scores - top)
            weight_sum = jnp.sum(weights, axis=-1, keepdims=True)
            total = total + dot(weights.astype(BF16), value * mask) / weight_sum
            stats = jnp.where(stat_lane == head, top + jnp.log(weight_sum), stats)
        att_ref[start : start + step_rows, :] = total.astype(BF16)
        lse_ref[start : start + step_rows, :] = stats


def attend(me, ids_row, ids_col, pieces, most):
    count = len(pieces)
    rows, wide = pieces[0].shape
    width = wide // 3
    length = count * rows
    step_rows = min(256, length)
    vmem = pl.BlockSpec(memory_space=pltpu.VMEM)
    return pl.pallas_call(
        functools.partial(attend_kernel, count, most, step_rows),
        in_specs=[pl.BlockSpec(memory_space=pltpu.SMEM)] + [vmem] * (2 + count),
        out_specs=[vmem] * 3,
        out_shape=[
            jax.ShapeDtypeStruct((length, width), BF16),
            jax.ShapeDtypeStruct((length, wide), BF16),
            jax.ShapeDtypeStruct((length, 128), F32),
        ],
        compiler_params=kernel_params(),
        cost_estimate=pl.CostEstimate(
            flops=4 * length * most * width * 4, bytes_accessed=4 * length * wide, transcendentals=0
        ),
        name="attend",
    )(me, ids_row, ids_col, *pieces)


def attend_back_kernel(
    count, most, step_rows, me_ref, ids_row_ref, ids_col_ref, cos_ref, right_ref, left_ref, *refs
):
    pieces = refs[:count]
    att_ref, all_ref, lse_ref, out_ref, sums_ref, grad_ref, dk_ref, dv_ref = refs[count:]
    rows, width = pieces[0].shape
    length = count * rows
    me = me_ref[0]
    for bits in range(count):
        place = pl.multiple_of((me ^ bits) * rows, rows)
        grad_ref[pl.ds(place, rows), :] = pieces[bits][...]
    dk_ref[...] = jnp.zeros_like(dk_ref)
    dv_ref[...] = jnp.zeros_like(dv_ref)
    ids_row = ids_row_ref[...]
    query_sum = jnp.zeros((1, width), F32)
    for start, first, stop in windows(length, most, step_rows):
        own = slice(start, start + step_rows)
        allowed = seen(start, first, stop, step_rows, ids_row, ids_col_ref)
        query = all_ref[own, 0:width]
        key = all_ref[first:stop, width : 2 * width]
        value = all_ref[first:stop, 2 * width : 3 * width]
        incoming = grad_ref[own, :]
        product = incoming.astype(F32) * att_ref[own, :].astype(F32)
        query_grad = jnp.zeros((step_rows, width), F32)
        key_grad = jnp.zeros((stop - first, width), F32)
        value_grad = jnp.zeros((stop - first, width), F32)
        for head in range(width // HD):
            mask32 = head_mask(width, head)
            mask = mask32.astype(BF16)
            delta = jnp.sum(product * mask32, axis=-1, keepdims=True)
            scores = dot_back(query * mask, key) * score_scale
            probability = jnp.where(
                allowed, jnp.exp(scores - lse_ref[own, head : head + 1]), 0.0
            )
            incoming_head = incoming * mask
            value_grad = value_grad + dot_rows(probability.astype(BF16), incoming_head)
            grad_prob = dot_back(incoming_head, value)
            grad_score = (probability * (grad_prob - delta) * score_scale).astype(BF16)
            query_grad = query_grad + dot(grad_score, key * mask)
            key_grad = key_grad + dot_rows(grad_score, query * mask)
        dk_ref[first:stop, :] += key_grad
        dv_ref[first:stop, :] += value_grad
        query_grad = turned(query_grad, cos_ref[own, :], -right_ref[own, :], -left_ref[own, :])
        query_sum = query_sum + jnp.sum(query_grad, axis=0, keepdims=True)
        out_ref[own, 0:width] = query_grad.astype(BF16)
    out_ref[:, width : 2 * width] = turned(
        dk_ref[...], cos_ref[...], -right_ref[...], -left_ref[...]
    ).astype(BF16)
    value_grad = dv_ref[...]
    out_ref[:, 2 * width : 3 * width] = value_grad.astype(BF16)
    value_sum = jnp.sum(value_grad, axis=0, keepdims=True)
    sums_ref[...] = jnp.concatenate(
        [query_sum, value_sum, jnp.zeros((6, width), F32)], axis=0
    )


def attend_back(me, ids_row, ids_col, tables, pieces, att, everything, lse, most):
    count = len(pieces)
    rows, width = pieces[0].shape
    length = count * rows
    step_rows = min(256, length)
    vmem = pl.BlockSpec(memory_space=pltpu.VMEM)
    return pl.pallas_call(
        functools.partial(attend_back_kernel, count, most, step_rows),
        in_specs=[pl.BlockSpec(memory_space=pltpu.SMEM)] + [vmem] * (8 + count),
        out_specs=[vmem] * 2,
        out_shape=[
            jax.ShapeDtypeStruct((length, 3 * width), BF16),
            jax.ShapeDtypeStruct((8, width), F32),
        ],
        scratch_shapes=[
            pltpu.VMEM((length, width), BF16),
            pltpu.VMEM((length, width), F32),
            pltpu.VMEM((length, width), F32),
        ],
        compiler_params=kernel_params(),
        cost_estimate=pl.CostEstimate(
            flops=10 * length * most * width * 4,
            bytes_accessed=16 * length * width,
            transcendentals=0,
        ),
        name="attend_back",
    )(me, ids_row, ids_col, *tables, *pieces, att, everything, lse)


def halve_kernel(chips, me_ref, matrix_ref, own_ref, other_ref):
    core = me_ref[0] % 2
    cols = matrix_ref.shape[1] // (2 * chips)
    for chip in range(chips):
        into = slice(chip * cols, (chip + 1) * cols)
        for out_ref, which in ((own_ref, core), (other_ref, 1 - core)):
            start = pl.multiple_of((2 * chip + which) * cols, cols)
            out_ref[:, into] = matrix_ref[:, pl.ds(start, cols)]


def halve(me, matrix, chips):
    rows, cols = matrix.shape
    vmem = pl.BlockSpec(memory_space=pltpu.VMEM)
    return pl.pallas_call(
        functools.partial(halve_kernel, chips),
        in_specs=[pl.BlockSpec(memory_space=pltpu.SMEM), vmem],
        out_specs=[vmem] * 2,
        out_shape=[jax.ShapeDtypeStruct((rows, cols // 2), BF16)] * 2,
        compiler_params=kernel_params(),
        cost_estimate=pl.CostEstimate(
            flops=0, bytes_accessed=4 * rows * cols, transcendentals=0
        ),
        name="halve",
    )(me, matrix)


def pack_kernel(qkv_ref, out_ref, packed_ref):
    head_cols = qkv_ref.shape[2]
    for which in range(3):
        packed_ref[:, which * head_cols : (which + 1) * head_cols] = qkv_ref[which].astype(BF16)
    packed_ref[:, 3 * head_cols : 4 * head_cols] = out_ref[...].T.astype(BF16)


def pack(w_qkv, w_out):
    _, rows, head_cols = w_qkv.shape
    vmem = pl.BlockSpec(memory_space=pltpu.VMEM)
    return pl.pallas_call(
        pack_kernel,
        in_specs=[vmem] * 2,
        out_specs=vmem,
        out_shape=jax.ShapeDtypeStruct((rows, 4 * head_cols), BF16),
        compiler_params=kernel_params(),
        name="pack",
    )(w_qkv, w_out)


def adam_kernel(leading, share_ref, master_ref, first_ref, second_ref, *outs):
    parts = master_ref.shape[0 if leading else 1]
    cols = master_ref.shape[2]
    for part in range(parts):
        spot = (part,) if leading else (slice(None), part)
        gradient = share_ref[:, part * cols : (part + 1) * cols].astype(F32)
        updates = adam_step(
            master_ref[spot], gradient, first_ref[spot], second_ref[spot], weight_decay
        )
        for out_ref, value in zip(outs, (gradient, *updates)):
            out_ref[spot] = value


def adam_parts(leading, share, *arrays):
    shape = arrays[0].shape
    rows, width = share.shape
    step_rows = max(
        size
        for size in range(16, rows + 1, 16)
        if rows % size == 0 and (size == 16 or size * width <= 100000)
    )
    if leading:
        block = pl.BlockSpec((shape[0], step_rows, shape[2]), lambda step: (0, step, 0))
    else:
        block = pl.BlockSpec((step_rows, shape[1], shape[2]), lambda step: (step, 0, 0))
    return pl.pallas_call(
        functools.partial(adam_kernel, leading),
        grid=(rows // step_rows,),
        in_specs=[pl.BlockSpec((step_rows, width), lambda step: (step, 0))] + [block] * 3,
        out_specs=[block] * 4,
        out_shape=[jax.ShapeDtypeStruct(shape, F32)] * 4,
        compiler_params=kernel_params(),
        cost_estimate=pl.CostEstimate(
            flops=0, bytes_accessed=30 * rows * width, transcendentals=0
        ),
        name="adam",
    )(share, *arrays)


def place_kernel(count, groups, parts, me_ref, *refs):
    pieces = refs[:count]
    out_ref = refs[count]
    rows = pieces[0].shape[0]
    width = pieces[0].shape[1] // parts
    for bits in range(count):
        source = me_ref[0] ^ bits
        row = pl.multiple_of(((source // groups) ^ me_ref[1]) * rows, rows)
        for part in range(parts):
            col = pl.multiple_of((part * groups + source % groups) * width, width)
            out_ref[pl.ds(row, rows), pl.ds(col, width)] = pieces[bits][
                :, part * width : (part + 1) * width
            ]


def place(places, pieces, groups, parts):
    count = len(pieces)
    rows, wide = pieces[0].shape
    vmem = pl.BlockSpec(memory_space=pltpu.VMEM)
    return pl.pallas_call(
        functools.partial(place_kernel, count, groups, parts),
        in_specs=[pl.BlockSpec(memory_space=pltpu.SMEM)] + [vmem] * count,
        out_specs=vmem,
        out_shape=jax.ShapeDtypeStruct((count // groups * rows, groups * wide), BF16),
        compiler_params=kernel_params(),
        cost_estimate=pl.CostEstimate(
            flops=0, bytes_accessed=4 * count * rows * wide, transcendentals=0
        ),
        name="place",
    )(places, *pieces)


def local(
    hidden,
    cotangent,
    doc_ids,
    w_qkv,
    w_out,
    w_gu,
    w_down,
    norm_vecs,
    first_qkv,
    first_out,
    first_gu,
    first_down,
    first_vecs,
    second_qkv,
    second_out,
    second_gu,
    second_down,
    second_vecs,
):
    ctx_size = lax.axis_size("ctx")
    ctx_place = lax.axis_index("ctx")
    shard_count = lax.axis_size("wsh")
    shard_place = lax.axis_index("wsh")
    tok_rows = hidden.shape[1]
    depth = hidden.shape[2]
    length = doc_ids.shape[1]
    most = length // 2
    head_cols = w_qkv.shape[2]
    unit_cols = w_gu.shape[2]
    own_rows = w_qkv.shape[0]
    groups = ctx_size // shard_count
    width = head_cols // groups
    ctx_scalar = ctx_place.astype(jnp.int32).reshape(1)
    places = jnp.stack([ctx_place, shard_place]).astype(jnp.int32)

    first_weights = pack(w_qkv.transpose(1, 0, 2), w_out)
    first_all = lax.all_gather(first_weights, "ctx", axis=0, tiled=True)
    gu_part = w_gu.astype(BF16).reshape(own_rows, 2 * unit_cols)
    gu_flat = lax.all_gather(gu_part, "ctx", axis=0, tiled=True)
    down_weight = lax.all_gather(w_down.astype(BF16), "ctx", axis=1, tiled=True)

    hidden_blocks = gather_rows(hidden[0], "wsh")
    cot_all = jnp.concatenate(gather_rows(cotangent[0], "wsh"), axis=0)

    own_seq = ctx_place // groups
    ids_own = lax.dynamic_slice_in_dim(doc_ids, own_seq, 1, 0)
    ids_col = ids_own.reshape(length, 1)
    positions = ctx_place * tok_rows + jnp.arange(tok_rows, dtype=jnp.int32)
    tables = rotary_tables(positions, width)
    tables_all = rotary_tables(jnp.arange(length, dtype=jnp.int32), width)

    own_vectors = jnp.pad(norm_vecs.astype(BF16).astype(F32).T, ((0, 2), (0, 0)))
    vectors = butterfly(
        lax.dynamic_update_slice(
            jnp.zeros((8, depth), F32), own_vectors, (0, ctx_place * own_rows)
        ),
        "ctx",
    )
    gain_one, shift_one, gain_two, shift_two = [vectors[row : row + 1] for row in range(4)]
    col_start = shard_place * head_cols
    bias_query = lax.dynamic_slice_in_dim(vectors[4:5], col_start, head_cols, 1)
    bias_value = lax.dynamic_slice_in_dim(vectors[5:6], col_start, head_cols, 1)
    qkv_flat = first_all[:, : 3 * head_cols]
    out_turned = first_all[:, 3 * head_cols :]

    gathered_one, projected = project(
        hidden_blocks, gain_one, shift_one, bias_query, bias_value, tables, first_all, groups
    )

    def exchange_out(array, bits):
        target = ctx_place ^ bits
        picked = lax.dynamic_slice(
            array,
            ((target // groups) ^ shard_place, target % groups, 0, 0),
            (1, 1) + array.shape[2:],
        )[0, 0]
        return picked if bits == 0 else swapped(picked, "ctx", bits)

    def exchange_back(array, bits):
        picked = lax.dynamic_slice_in_dim(array, (ctx_place ^ bits) * tok_rows, tok_rows, 0)
        return picked if bits == 0 else swapped(picked, "ctx", bits)

    pieces = [exchange_out(projected, bits) for bits in range(ctx_size)]
    att_own, qkv_own, log_sums = attend(ctx_scalar, ids_own, ids_col, pieces, most)
    attended = place(
        places, [exchange_back(att_own, bits) for bits in range(ctx_size)], groups, 1
    )

    def row_blocks(matrix):
        return [
            matrix[place_row * tok_rows : (place_row + 1) * tok_rows]
            for place_row in range(shard_count)
        ]

    attn_terms = dot_back(attended, out_turned).astype(BF16)
    middle = hidden[0].astype(F32) + scatter_sum(row_blocks(attn_terms), "wsh")
    normed_two, hat_two, inverse_two = layer_norm(middle, gain_two, shift_two)
    gathered_two = jnp.concatenate(gather_rows(normed_two.astype(BF16), "wsh"), axis=0)
    gate_up = dot(gathered_two, gu_flat)
    gate_part = gate_up[:, :unit_cols]
    activated = (gate_part * jax.nn.sigmoid(gate_part) * gate_up[:, unit_cols:]).astype(BF16)
    share_down = chip_scatter(lambda half: dot_rows(activated, half), halve(ctx_scalar, cot_all, ctx_size // 2), 1)

    gate_up = lax.optimization_barrier(gate_up)
    gate_part = gate_up[:, :unit_cols]
    up_part = gate_up[:, unit_cols:]
    sigmoid_gate = jax.nn.sigmoid(gate_part)
    grad_act = dot_back(cot_all, down_weight)
    grad_gate = grad_act * up_part * sigmoid_gate * (1.0 + gate_part * (1.0 - sigmoid_gate))
    grad_up = grad_act * gate_part * sigmoid_gate
    grad_gate_up = jnp.concatenate([grad_gate, grad_up], axis=1).astype(BF16)
    share_gu = chip_scatter(lambda half: dot_rows(half, grad_gate_up), halve(ctx_scalar, gathered_two, ctx_size // 2), 0)
    normed_two_terms = dot_back(grad_gate_up, gu_flat).astype(BF16)
    grad_normed_two = scatter_sum(row_blocks(normed_two_terms), "wsh")
    grad_middle, grad_gain_two, grad_shift_two = norm_back(
        grad_normed_two, hat_two, inverse_two, gain_two
    )
    grad_middle = grad_middle + cotangent[0].astype(F32)
    middle_all = jnp.concatenate(gather_rows(grad_middle.astype(BF16), "wsh"), axis=0)
    share_out = chip_scatter(lambda half: dot_rows(attended, half), halve(ctx_scalar, middle_all, ctx_size // 2), 1)
    grad_att = dot(middle_all, out_turned).astype(BF16)

    def exchange_grad(bits):
        target = ctx_place ^ bits
        row = ((target // groups) ^ shard_place) * tok_rows
        picked = lax.dynamic_slice(
            grad_att, (row, target % groups * width), (tok_rows, width)
        )
        return picked if bits == 0 else swapped(picked, "ctx", bits)

    grad_pieces = [exchange_grad(bits) for bits in range(ctx_size)]
    grad_own, bias_sums = attend_back(
        ctx_scalar, ids_own, ids_col, tables_all, grad_pieces, att_own, qkv_own, log_sums, most
    )
    grad_rows = place(
        places, [exchange_back(grad_own, bits) for bits in range(ctx_size)], groups, 3
    )
    share_qkv = chip_scatter(lambda half: dot_rows(half, grad_rows), halve(ctx_scalar, gathered_one, ctx_size // 2), 0)

    late_activated, late_middle, _ = lax.optimization_barrier((activated, middle, grad_rows))
    ffn_terms = dot(late_activated, down_weight).astype(BF16)
    block_out = (late_middle + scatter_sum(row_blocks(ffn_terms), "wsh")).astype(BF16)

    normed_one_terms = dot_back(grad_rows, qkv_flat).astype(BF16)
    grad_normed_one = scatter_sum(row_blocks(normed_one_terms), "wsh")
    _, hat_one, inverse_one = layer_norm(hidden[0].astype(F32), gain_one, shift_one)
    grad_input, grad_gain_one, grad_shift_one = norm_back(
        grad_normed_one, hat_one, inverse_one, gain_one
    )
    grad_input = grad_input + grad_middle

    bias_start = shard_place * head_cols + (ctx_place % groups) * width
    bias_rows = lax.dynamic_update_slice(
        jnp.zeros((2, depth), F32), bias_sums[:2], (0, bias_start)
    )
    vec_terms = jnp.concatenate(
        [
            grad_gain_one[None],
            grad_shift_one[None],
            grad_gain_two[None],
            grad_shift_two[None],
            bias_rows,
            jnp.zeros((2, depth), F32),
        ],
        axis=0,
    )
    vec_sums = butterfly(butterfly(vec_terms, "ctx"), "wsh")
    share_vecs = lax.dynamic_slice_in_dim(vec_sums, ctx_place * own_rows, own_rows, 1).T[:, :6]

    share_qkv, new_qkv, new_first_qkv, new_second_qkv = [
        array.transpose(1, 0, 2)
        for array in adam_parts(
            True,
            share_qkv,
            *[array.transpose(1, 0, 2) for array in (w_qkv, first_qkv, second_qkv)],
        )
    ]
    share_gu, new_gu, new_first_gu, new_second_gu = adam_parts(
        False, share_gu, w_gu, first_gu, second_gu
    )
    share_down, new_down, new_first_down, new_second_down = [
        array[0]
        for array in adam_parts(True, share_down, w_down[None], first_down[None], second_down[None])
    ]
    share_out, new_out, new_first_out, new_second_out = [
        array[0]
        for array in adam_parts(
            True, share_out, w_out[None], first_out[None], second_out[None]
        )
    ]
    new_vecs, new_first_vecs, new_second_vecs = adam_step(
        norm_vecs, share_vecs, first_vecs, second_vecs, 0.0
    )
    return (
        block_out[None],
        grad_input[None],
        share_qkv,
        share_out,
        share_gu,
        share_down,
        share_vecs,
        new_qkv,
        new_out,
        new_gu,
        new_down,
        new_vecs,
        new_first_qkv,
        new_first_out,
        new_first_gu,
        new_first_down,
        new_first_vecs,
        new_second_qkv,
        new_second_out,
        new_second_gu,
        new_second_down,
        new_second_vecs,
    )


def solution(mesh):
    rows = P("wsh", "ctx", None)
    weights = (
        P("ctx", None, "wsh"),
        P("wsh", "ctx"),
        P("ctx", None, "wsh"),
        P("wsh", "ctx"),
        P("ctx", None),
    )
    return jax.shard_map(
        local,
        mesh=mesh,
        in_specs=(rows, rows, P()) + weights * 3,
        out_specs=(rows, rows) + weights * 4,
        check_vma=False,
    )
```

```python
import functools

import jax
import jax.numpy as jnp
from jax import lax
from jax.experimental import pallas as pl
from jax.experimental.pallas import tpu as pltpu
from jax.sharding import PartitionSpec as P


HD = 64
ROT = 16
STEP = 4


learn_rate = 0.005
beta_first = 0.9
beta_second = 0.95
adam_epsilon = 1e-08
weight_decay = 0.1
norm_epsilon = 1e-05
masked_score = -1e30
score_scale = HD ** (-0.5)
F32 = jnp.float32
BF16 = jnp.bfloat16


def swapped(value, axis, bits):
    count = lax.axis_size(axis)
    return lax.ppermute(value, axis, [(source, source ^ bits) for source in range(count)])


def gather_rows(block, axis):
    count = lax.axis_size(axis)
    return [block] + [swapped(block, axis, bits) for bits in range(1, count)]


def scatter_sum(blocks, axis):
    total = blocks[0].astype(F32)
    for bits in range(1, len(blocks)):
        total = total + swapped(blocks[bits], axis, bits).astype(F32)
    return total


def butterfly(value, axis):
    count = lax.axis_size(axis)
    bits = 1
    while bits < count:
        value = value + swapped(value, axis, bits)
        bits *= 2
    return value


def core_sum(product, halves):
    own, other = halves
    sent = product(other).astype(BF16)
    return (product(own) + swapped(sent, "ctx", 1).astype(F32)).astype(BF16)


def chip_scatter(total, axis):
    count = lax.axis_size("ctx")
    return lax.psum_scatter(
        total,
        "ctx",
        scatter_dimension=axis,
        tiled=True,
        axis_index_groups=[list(range(first, count, 2)) for first in range(2)],
    )


def layer_norm(matrix, gain_vec, shift_vec):
    centre = matrix - jnp.mean(matrix, axis=-1, keepdims=True)
    inverse = lax.rsqrt(jnp.mean(centre * centre, axis=-1, keepdims=True) + norm_epsilon)
    normed = centre * inverse
    return (normed * gain_vec + shift_vec, normed, inverse)


def norm_back(incoming, normed, inverse, gain_vec):
    scaled = incoming * gain_vec
    inner = (
        scaled
        - jnp.mean(scaled, axis=-1, keepdims=True)
        - normed * jnp.mean(scaled * normed, axis=-1, keepdims=True)
    )
    return (inner * inverse, jnp.sum(incoming * normed, axis=0), jnp.sum(incoming, axis=0))


def rotary_tables(positions, width):
    half_rot = ROT // 2
    lane = jnp.arange(width, dtype=jnp.int32) % HD
    frequency = 10000.0 ** (-2.0 * (lane % half_rot).astype(F32) / ROT)
    angles = positions.astype(F32)[:, None] * frequency[None, :]
    turning = (lane < ROT)[None, :]
    low_lane = (lane < half_rot)[None, :]
    cosine = jnp.where(turning, jnp.cos(angles), 1.0)
    sine = jnp.where(turning, jnp.sin(angles), 0.0)
    return cosine, jnp.where(low_lane, -sine, 0.0), jnp.where(low_lane, 0.0, sine)


def turned(value, cosine, from_right, from_left):
    width = value.shape[-1]
    half_rot = ROT // 2
    return (
        value * cosine
        + pltpu.roll(value, width - half_rot, 1) * from_right
        + pltpu.roll(value, half_rot, 1) * from_left
    )


def dot_rows(left_side, right_side):
    return lax.dot_general(
        left_side, right_side, (((0,), (0,)), ((), ())), preferred_element_type=F32
    )


def dot_back(left_side, right_side):
    return lax.dot_general(
        left_side, right_side, (((1,), (1,)), ((), ())), preferred_element_type=F32
    )


def dot(left_side, right_side):
    return jnp.dot(left_side, right_side, preferred_element_type=F32)


def adam_step(master, gradient, first_moment, second_moment, decay_rate):
    moment_one = beta_first * first_moment + (1.0 - beta_first) * gradient
    moment_two = beta_second * second_moment + (1.0 - beta_second) * gradient * gradient
    corrected = moment_one / (1.0 - beta_first**STEP)
    spread = jnp.sqrt(moment_two / (1.0 - beta_second**STEP))
    updated = master - learn_rate * (corrected / (spread + adam_epsilon) + decay_rate * master)
    return (updated, moment_one, moment_two)


def kernel_params(megabytes=48):
    return pltpu.CompilerParams(vmem_limit_bytes=megabytes * 1024 * 1024)


def project_kernel(count, *refs):
    blocks = refs[:count]
    gain, shift, bias_q, bias_v, cosine, from_right, from_left, wq, wk, wv = refs[count : count + 10]
    normed_ref, out_ref = refs[count + 10 :]
    rows, _ = blocks[0].shape
    width = wq.shape[1]

    @pl.when(pl.program_id(0) == 0)
    def _():
        for place in range(count):
            value, _, _ = layer_norm(blocks[place][...].astype(F32), gain[...], shift[...])
            normed_ref[place * rows : (place + 1) * rows, :] = value.astype(BF16)

    for which, weight in enumerate((wq, wk, wv)):
        result = dot(normed_ref[...], weight[...])
        if which == 0:
            result = result + bias_q[...]
        if which == 2:
            result = result + bias_v[...]
        for place in range(count):
            part = result[place * rows : (place + 1) * rows]
            if which < 2:
                part = turned(part, cosine[...], from_right[...], from_left[...])
            out_ref[place, 0, :, which * width : (which + 1) * width] = part.astype(BF16)


def project(blocks, gain, shift, bias_q, bias_v, tables, weights, groups):
    count = len(blocks)
    rows, depth = blocks[0].shape
    head_cols = bias_q.shape[1]
    width = head_cols // groups

    def whole(array):
        return pl.BlockSpec(array.shape, lambda g: (0, 0))

    def column(first):
        return pl.BlockSpec((depth, width), lambda g: (0, first * groups + g))

    operands = [*blocks, gain, shift, bias_q, bias_v, *tables]
    specs = [whole(block) for block in blocks] + [whole(gain), whole(shift)]
    specs += [pl.BlockSpec((1, width), lambda g: (0, g))] * 2
    specs += [whole(table) for table in tables]
    specs += [column(0), column(1), column(2)]
    return pl.pallas_call(
        functools.partial(project_kernel, count),
        grid=(groups,),
        in_specs=specs,
        out_specs=[
            pl.BlockSpec((count * rows, depth), lambda g: (0, 0)),
            pl.BlockSpec((count, 1, rows, 3 * width), lambda g: (0, g, 0, 0)),
        ],
        out_shape=[
            jax.ShapeDtypeStruct((count * rows, depth), BF16),
            jax.ShapeDtypeStruct((count, groups, rows, 3 * width), BF16),
        ],
        compiler_params=kernel_params(),
        cost_estimate=pl.CostEstimate(
            flops=2 * count * rows * depth * 3 * head_cols,
            bytes_accessed=2 * depth * 3 * head_cols + 4 * count * rows * depth,
            transcendentals=0,
        ),
        name="project",
    )(*operands, weights, weights, weights)


def windows(length, most, rows):
    for start in range(0, length, rows):
        first = max(0, (start - (most - 1)) // rows * rows)
        yield start, first, start + rows


def seen(start, first, stop, rows, ids_row, ids_col):
    query_pos = start + lax.broadcasted_iota(jnp.int32, (rows, stop - first), 0)
    key_pos = first + lax.broadcasted_iota(jnp.int32, (rows, stop - first), 1)
    same = ids_row[:, first:stop] == ids_col[start : start + rows, :]
    return (key_pos <= query_pos) & same


def head_mask(width, head):
    lane = lax.broadcasted_iota(jnp.int32, (1, width), 1) // HD
    return jnp.where(lane == head, 1.0, 0.0).astype(F32)


def attend_kernel(count, most, step_rows, me_ref, ids_row_ref, ids_col_ref, *refs):
    pieces = refs[:count]
    att_ref, all_ref, lse_ref = refs[count:]
    rows = pieces[0].shape[0]
    width = pieces[0].shape[1] // 3
    length = count * rows
    me = me_ref[0]
    for bits in range(count):
        place = pl.multiple_of((me ^ bits) * rows, rows)
        all_ref[pl.ds(place, rows), :] = pieces[bits][...]
    ids_row = ids_row_ref[...]
    stat_lane = lax.broadcasted_iota(jnp.int32, (step_rows, 128), 1)
    for start, first, stop in windows(length, most, step_rows):
        allowed = seen(start, first, stop, step_rows, ids_row, ids_col_ref)
        query = all_ref[start : start + step_rows, 0:width]
        key = all_ref[first:stop, width : 2 * width]
        value = all_ref[first:stop, 2 * width : 3 * width]
        stats = jnp.zeros((step_rows, 128), F32)
        total = jnp.zeros((step_rows, width), F32)
        for head in range(width // HD):
            mask = head_mask(width, head).astype(BF16)
            scores = dot_back(query * mask, key) * score_scale
            scores = jnp.where(allowed, scores, masked_score)
            top = jnp.max(scores, axis=-1, keepdims=True)
            weights = jnp.exp(scores - top)
            weight_sum = jnp.sum(weights, axis=-1, keepdims=True)
            total = total + dot(weights.astype(BF16), value * mask) / weight_sum
            stats = jnp.where(stat_lane == head, top + jnp.log(weight_sum), stats)
        att_ref[start : start + step_rows, :] = total.astype(BF16)
        lse_ref[start : start + step_rows, :] = stats


def attend(me, ids_row, ids_col, pieces, most):
    count = len(pieces)
    rows, wide = pieces[0].shape
    width = wide // 3
    length = count * rows
    step_rows = min(256, length)
    vmem = pl.BlockSpec(memory_space=pltpu.VMEM)
    return pl.pallas_call(
        functools.partial(attend_kernel, count, most, step_rows),
        in_specs=[pl.BlockSpec(memory_space=pltpu.SMEM)] + [vmem] * (2 + count),
        out_specs=[vmem] * 3,
        out_shape=[
            jax.ShapeDtypeStruct((length, width), BF16),
            jax.ShapeDtypeStruct((length, wide), BF16),
            jax.ShapeDtypeStruct((length, 128), F32),
        ],
        compiler_params=kernel_params(),
        cost_estimate=pl.CostEstimate(
            flops=4 * length * most * width * 4, bytes_accessed=4 * length * wide, transcendentals=0
        ),
        name="attend",
    )(me, ids_row, ids_col, *pieces)


def attend_back_kernel(
    count, most, step_rows, me_ref, ids_row_ref, ids_col_ref, cos_ref, right_ref, left_ref, *refs
):
    pieces = refs[:count]
    att_ref, all_ref, lse_ref, out_ref, sums_ref, grad_ref, dk_ref, dv_ref = refs[count:]
    rows, width = pieces[0].shape
    length = count * rows
    me = me_ref[0]
    for bits in range(count):
        place = pl.multiple_of((me ^ bits) * rows, rows)
        grad_ref[pl.ds(place, rows), :] = pieces[bits][...]
    dk_ref[...] = jnp.zeros_like(dk_ref)
    dv_ref[...] = jnp.zeros_like(dv_ref)
    ids_row = ids_row_ref[...]
    query_sum = jnp.zeros((1, width), F32)
    for start, first, stop in windows(length, most, step_rows):
        own = slice(start, start + step_rows)
        allowed = seen(start, first, stop, step_rows, ids_row, ids_col_ref)
        query = all_ref[own, 0:width]
        key = all_ref[first:stop, width : 2 * width]
        value = all_ref[first:stop, 2 * width : 3 * width]
        incoming = grad_ref[own, :]
        product = incoming.astype(F32) * att_ref[own, :].astype(F32)
        query_grad = jnp.zeros((step_rows, width), F32)
        key_grad = jnp.zeros((stop - first, width), F32)
        value_grad = jnp.zeros((stop - first, width), F32)
        for head in range(width // HD):
            mask32 = head_mask(width, head)
            mask = mask32.astype(BF16)
            delta = jnp.sum(product * mask32, axis=-1, keepdims=True)
            scores = dot_back(query * mask, key) * score_scale
            probability = jnp.where(
                allowed, jnp.exp(scores - lse_ref[own, head : head + 1]), 0.0
            )
            incoming_head = incoming * mask
            value_grad = value_grad + dot_rows(probability.astype(BF16), incoming_head)
            grad_prob = dot_back(incoming_head, value)
            grad_score = (probability * (grad_prob - delta) * score_scale).astype(BF16)
            query_grad = query_grad + dot(grad_score, key * mask)
            key_grad = key_grad + dot_rows(grad_score, query * mask)
        dk_ref[first:stop, :] += key_grad
        dv_ref[first:stop, :] += value_grad
        query_grad = turned(query_grad, cos_ref[own, :], -right_ref[own, :], -left_ref[own, :])
        query_sum = query_sum + jnp.sum(query_grad, axis=0, keepdims=True)
        out_ref[own, 0:width] = query_grad.astype(BF16)
    out_ref[:, width : 2 * width] = turned(
        dk_ref[...], cos_ref[...], -right_ref[...], -left_ref[...]
    ).astype(BF16)
    value_grad = dv_ref[...]
    out_ref[:, 2 * width : 3 * width] = value_grad.astype(BF16)
    value_sum = jnp.sum(value_grad, axis=0, keepdims=True)
    sums_ref[...] = jnp.concatenate(
        [query_sum, value_sum, jnp.zeros((6, width), F32)], axis=0
    )


def attend_back(me, ids_row, ids_col, tables, pieces, att, everything, lse, most):
    count = len(pieces)
    rows, width = pieces[0].shape
    length = count * rows
    step_rows = min(256, length)
    vmem = pl.BlockSpec(memory_space=pltpu.VMEM)
    return pl.pallas_call(
        functools.partial(attend_back_kernel, count, most, step_rows),
        in_specs=[pl.BlockSpec(memory_space=pltpu.SMEM)] + [vmem] * (8 + count),
        out_specs=[vmem] * 2,
        out_shape=[
            jax.ShapeDtypeStruct((length, 3 * width), BF16),
            jax.ShapeDtypeStruct((8, width), F32),
        ],
        scratch_shapes=[
            pltpu.VMEM((length, width), BF16),
            pltpu.VMEM((length, width), F32),
            pltpu.VMEM((length, width), F32),
        ],
        compiler_params=kernel_params(),
        cost_estimate=pl.CostEstimate(
            flops=10 * length * most * width * 4,
            bytes_accessed=16 * length * width,
            transcendentals=0,
        ),
        name="attend_back",
    )(me, ids_row, ids_col, *tables, *pieces, att, everything, lse)


def halve_kernel(chips, me_ref, matrix_ref, own_ref, other_ref):
    core = me_ref[0] % 2
    cols = matrix_ref.shape[1] // (2 * chips)
    for chip in range(chips):
        into = slice(chip * cols, (chip + 1) * cols)
        for out_ref, which in ((own_ref, core), (other_ref, 1 - core)):
            start = pl.multiple_of((2 * chip + which) * cols, cols)
            out_ref[:, into] = matrix_ref[:, pl.ds(start, cols)]


def halve(me, matrix, chips):
    rows, cols = matrix.shape
    vmem = pl.BlockSpec(memory_space=pltpu.VMEM)
    return pl.pallas_call(
        functools.partial(halve_kernel, chips),
        in_specs=[pl.BlockSpec(memory_space=pltpu.SMEM), vmem],
        out_specs=[vmem] * 2,
        out_shape=[jax.ShapeDtypeStruct((rows, cols // 2), BF16)] * 2,
        compiler_params=kernel_params(),
        cost_estimate=pl.CostEstimate(
            flops=0, bytes_accessed=4 * rows * cols, transcendentals=0
        ),
        name="halve",
    )(me, matrix)


def join_kernel(blocks, left_ref, rows_ref, other_ref, out_sum_ref, out_ref):
    @pl.when(pl.program_id(0) < blocks)
    def _():
        kept = dot(left_ref[...], rows_ref[...]) + other_ref[...].astype(F32)
        out_ref[...] = kept.astype(BF16)

    @pl.when(pl.program_id(0) >= blocks)
    def _():
        out_ref[...] = out_sum_ref[...]


def join(left, rows, other, out_sum, width):
    half, count = left.shape
    blocks = rows.shape[1] // width
    total = blocks + out_sum.shape[1] // width
    return pl.pallas_call(
        functools.partial(join_kernel, blocks),
        grid=(total,),
        in_specs=[
            pl.BlockSpec((half, count), lambda b: (0, 0)),
            pl.BlockSpec((count, width), lambda b: (0, jnp.minimum(b, blocks - 1))),
            pl.BlockSpec((half, width), lambda b: (0, jnp.minimum(b, blocks - 1))),
            pl.BlockSpec((half, width), lambda b: (0, jnp.maximum(b - blocks, 0))),
        ],
        out_specs=pl.BlockSpec((half, width), lambda b: (0, b)),
        out_shape=jax.ShapeDtypeStruct((half, total * width), BF16),
        compiler_params=kernel_params(),
        cost_estimate=pl.CostEstimate(
            flops=2 * half * count * blocks * width,
            bytes_accessed=4 * half * total * width,
            transcendentals=0,
        ),
        name="join",
    )(left, rows, other, out_sum)


def pack_kernel(qkv_ref, out_ref, packed_ref):
    head_cols = qkv_ref.shape[2]
    for which in range(3):
        packed_ref[:, which * head_cols : (which + 1) * head_cols] = qkv_ref[which].astype(BF16)
    packed_ref[:, 3 * head_cols : 4 * head_cols] = out_ref[...].T.astype(BF16)


def pack(w_qkv, w_out):
    _, rows, head_cols = w_qkv.shape
    vmem = pl.BlockSpec(memory_space=pltpu.VMEM)
    return pl.pallas_call(
        pack_kernel,
        in_specs=[vmem] * 2,
        out_specs=vmem,
        out_shape=jax.ShapeDtypeStruct((rows, 4 * head_cols), BF16),
        compiler_params=kernel_params(),
        name="pack",
    )(w_qkv, w_out)


def adam_turned_kernel(share_ref, master_ref, first_ref, second_ref, *outs):
    gradient = share_ref[...].astype(F32).T
    updates = adam_step(
        master_ref[...], gradient, first_ref[...], second_ref[...], weight_decay
    )
    for out_ref, value in zip(outs, (gradient, *updates)):
        out_ref[...] = value


def adam_turned(share, *arrays):
    heads, own = arrays[0].shape
    whole = pl.BlockSpec((heads, own), lambda step: (0, 0))
    return pl.pallas_call(
        adam_turned_kernel,
        grid=(1,),
        in_specs=[pl.BlockSpec((own, heads), lambda step: (0, 3))] + [whole] * 3,
        out_specs=[whole] * 4,
        out_shape=[jax.ShapeDtypeStruct((heads, own), F32)] * 4,
        compiler_params=kernel_params(),
        cost_estimate=pl.CostEstimate(
            flops=0, bytes_accessed=30 * heads * own, transcendentals=0
        ),
        name="adam_turned",
    )(share, *arrays)


def adam_kernel(leading, share_ref, master_ref, first_ref, second_ref, *outs):
    parts = master_ref.shape[0 if leading else 1]
    cols = master_ref.shape[2]
    for part in range(parts):
        spot = (part,) if leading else (slice(None), part)
        gradient = share_ref[:, part * cols : (part + 1) * cols].astype(F32)
        updates = adam_step(
            master_ref[spot], gradient, first_ref[spot], second_ref[spot], weight_decay
        )
        for out_ref, value in zip(outs, (gradient, *updates)):
            out_ref[spot] = value


def adam_parts(leading, share, *arrays):
    shape = arrays[0].shape
    rows = share.shape[0]
    width = arrays[0].size // rows
    step_rows = max(
        size
        for size in range(16, rows + 1, 16)
        if rows % size == 0 and (size == 16 or size * width <= 100000)
    )
    if leading:
        block = pl.BlockSpec((shape[0], step_rows, shape[2]), lambda step: (0, step, 0))
    else:
        block = pl.BlockSpec((step_rows, shape[1], shape[2]), lambda step: (step, 0, 0))
    return pl.pallas_call(
        functools.partial(adam_kernel, leading),
        grid=(rows // step_rows,),
        in_specs=[pl.BlockSpec((step_rows, width), lambda step: (step, 0))] + [block] * 3,
        out_specs=[block] * 4,
        out_shape=[jax.ShapeDtypeStruct(shape, F32)] * 4,
        compiler_params=kernel_params(),
        cost_estimate=pl.CostEstimate(
            flops=0, bytes_accessed=30 * rows * width, transcendentals=0
        ),
        name="adam",
    )(share, *arrays)


def place_kernel(count, groups, parts, me_ref, *refs):
    pieces = refs[:count]
    out_ref = refs[count]
    rows = pieces[0].shape[0]
    width = pieces[0].shape[1] // parts
    for bits in range(count):
        source = me_ref[0] ^ bits
        row = pl.multiple_of(((source // groups) ^ me_ref[1]) * rows, rows)
        for part in range(parts):
            col = pl.multiple_of((part * groups + source % groups) * width, width)
            out_ref[pl.ds(row, rows), pl.ds(col, width)] = pieces[bits][
                :, part * width : (part + 1) * width
            ]


def place(places, pieces, groups, parts):
    count = len(pieces)
    rows, wide = pieces[0].shape
    vmem = pl.BlockSpec(memory_space=pltpu.VMEM)
    return pl.pallas_call(
        functools.partial(place_kernel, count, groups, parts),
        in_specs=[pl.BlockSpec(memory_space=pltpu.SMEM)] + [vmem] * count,
        out_specs=vmem,
        out_shape=jax.ShapeDtypeStruct((count // groups * rows, groups * wide), BF16),
        compiler_params=kernel_params(),
        cost_estimate=pl.CostEstimate(
            flops=0, bytes_accessed=4 * count * rows * wide, transcendentals=0
        ),
        name="place",
    )(places, *pieces)


def local(
    hidden,
    cotangent,
    doc_ids,
    w_qkv,
    w_out,
    w_gu,
    w_down,
    norm_vecs,
    first_qkv,
    first_out,
    first_gu,
    first_down,
    first_vecs,
    second_qkv,
    second_out,
    second_gu,
    second_down,
    second_vecs,
):
    ctx_size = lax.axis_size("ctx")
    ctx_place = lax.axis_index("ctx")
    shard_count = lax.axis_size("wsh")
    shard_place = lax.axis_index("wsh")
    tok_rows = hidden.shape[1]
    depth = hidden.shape[2]
    length = doc_ids.shape[1]
    most = length // 2
    head_cols = w_qkv.shape[2]
    unit_cols = w_gu.shape[2]
    own_rows = w_qkv.shape[0]
    groups = ctx_size // shard_count
    width = head_cols // groups
    ctx_scalar = ctx_place.astype(jnp.int32).reshape(1)
    places = jnp.stack([ctx_place, shard_place]).astype(jnp.int32)

    first_weights = pack(w_qkv.transpose(1, 0, 2), w_out)
    first_all = lax.all_gather(first_weights, "ctx", axis=0, tiled=True)
    gu_part = w_gu.astype(BF16).reshape(own_rows, 2 * unit_cols)
    gu_flat = lax.all_gather(gu_part, "ctx", axis=0, tiled=True)
    down_weight = lax.all_gather(w_down.astype(BF16), "ctx", axis=1, tiled=True)

    hidden_blocks = gather_rows(hidden[0], "wsh")
    cot_all = jnp.concatenate(gather_rows(cotangent[0], "wsh"), axis=0)

    own_seq = ctx_place // groups
    ids_own = lax.dynamic_slice_in_dim(doc_ids, own_seq, 1, 0)
    ids_col = ids_own.reshape(length, 1)
    positions = ctx_place * tok_rows + jnp.arange(tok_rows, dtype=jnp.int32)
    tables = rotary_tables(positions, width)
    tables_all = rotary_tables(jnp.arange(length, dtype=jnp.int32), width)

    own_vectors = jnp.pad(norm_vecs.astype(BF16).astype(F32).T, ((0, 2), (0, 0)))
    vectors = butterfly(
        lax.dynamic_update_slice(
            jnp.zeros((8, depth), F32), own_vectors, (0, ctx_place * own_rows)
        ),
        "ctx",
    )
    gain_one, shift_one, gain_two, shift_two = [vectors[row : row + 1] for row in range(4)]
    col_start = shard_place * head_cols
    bias_query = lax.dynamic_slice_in_dim(vectors[4:5], col_start, head_cols, 1)
    bias_value = lax.dynamic_slice_in_dim(vectors[5:6], col_start, head_cols, 1)
    qkv_flat = first_all[:, : 3 * head_cols]
    out_turned = first_all[:, 3 * head_cols :]

    gathered_one, projected = project(
        hidden_blocks, gain_one, shift_one, bias_query, bias_value, tables, first_all, groups
    )

    def exchange_out(array, bits):
        target = ctx_place ^ bits
        picked = lax.dynamic_slice(
            array,
            ((target // groups) ^ shard_place, target % groups, 0, 0),
            (1, 1) + array.shape[2:],
        )[0, 0]
        return picked if bits == 0 else swapped(picked, "ctx", bits)

    def exchange_back(array, bits):
        picked = lax.dynamic_slice_in_dim(array, (ctx_place ^ bits) * tok_rows, tok_rows, 0)
        return picked if bits == 0 else swapped(picked, "ctx", bits)

    pieces = [exchange_out(projected, bits) for bits in range(ctx_size)]
    att_own, qkv_own, log_sums = attend(ctx_scalar, ids_own, ids_col, pieces, most)
    attended = place(
        places, [exchange_back(att_own, bits) for bits in range(ctx_size)], groups, 1
    )

    def row_blocks(matrix):
        return [
            matrix[place_row * tok_rows : (place_row + 1) * tok_rows]
            for place_row in range(shard_count)
        ]

    attn_terms = dot_back(attended, out_turned).astype(BF16)
    middle = hidden[0].astype(F32) + scatter_sum(row_blocks(attn_terms), "wsh")
    normed_two, hat_two, inverse_two = layer_norm(middle, gain_two, shift_two)
    gathered_two = jnp.concatenate(gather_rows(normed_two.astype(BF16), "wsh"), axis=0)
    gate_up = dot(gathered_two, gu_flat)
    gate_part = gate_up[:, :unit_cols]
    activated = (gate_part * jax.nn.sigmoid(gate_part) * gate_up[:, unit_cols:]).astype(BF16)
    down_sum = core_sum(
        lambda half: dot_rows(activated, half), halve(ctx_scalar, cot_all, ctx_size // 2)
    )
    share_down = chip_scatter(down_sum, 1)

    gate_up = lax.optimization_barrier(gate_up)
    gate_part = gate_up[:, :unit_cols]
    up_part = gate_up[:, unit_cols:]
    sigmoid_gate = jax.nn.sigmoid(gate_part)
    grad_act = dot_back(cot_all, down_weight)
    grad_gate = grad_act * up_part * sigmoid_gate * (1.0 + gate_part * (1.0 - sigmoid_gate))
    grad_up = grad_act * gate_part * sigmoid_gate
    grad_gate_up = jnp.concatenate([grad_gate, grad_up], axis=1).astype(BF16)
    gu_sum = core_sum(
        lambda half: dot_rows(half, grad_gate_up),
        halve(ctx_scalar, gathered_two, ctx_size // 2),
    )
    share_gu = chip_scatter(gu_sum, 0)
    normed_two_terms = dot_back(grad_gate_up, gu_flat).astype(BF16)
    grad_normed_two = scatter_sum(row_blocks(normed_two_terms), "wsh")
    grad_middle, grad_gain_two, grad_shift_two = norm_back(
        grad_normed_two, hat_two, inverse_two, gain_two
    )
    grad_middle = grad_middle + cotangent[0].astype(F32)
    middle_all = jnp.concatenate(gather_rows(grad_middle.astype(BF16), "wsh"), axis=0)
    out_sum = core_sum(
        lambda half: dot_rows(half, attended), halve(ctx_scalar, middle_all, ctx_size // 2)
    )
    grad_att = dot(middle_all, out_turned).astype(BF16)

    def exchange_grad(bits):
        target = ctx_place ^ bits
        row = ((target // groups) ^ shard_place) * tok_rows
        picked = lax.dynamic_slice(
            grad_att, (row, target % groups * width), (tok_rows, width)
        )
        return picked if bits == 0 else swapped(picked, "ctx", bits)

    grad_pieces = [exchange_grad(bits) for bits in range(ctx_size)]
    grad_own, bias_sums = attend_back(
        ctx_scalar, ids_own, ids_col, tables_all, grad_pieces, att_own, qkv_own, log_sums, most
    )
    grad_rows = place(
        places, [exchange_back(grad_own, bits) for bits in range(ctx_size)], groups, 3
    )
    own_one, other_one = halve(ctx_scalar, gathered_one, ctx_size // 2)
    sent_qkv = dot_rows(other_one, grad_rows).astype(BF16)
    first_sum = join(own_one.T, grad_rows, swapped(sent_qkv, "ctx", 1), out_sum, width)
    share_first = chip_scatter(first_sum, 0)

    late_activated, late_middle, _ = lax.optimization_barrier((activated, middle, grad_rows))
    ffn_terms = dot(late_activated, down_weight).astype(BF16)
    block_out = (late_middle + scatter_sum(row_blocks(ffn_terms), "wsh")).astype(BF16)

    normed_one_terms = dot_back(grad_rows, qkv_flat).astype(BF16)
    grad_normed_one = scatter_sum(row_blocks(normed_one_terms), "wsh")
    _, hat_one, inverse_one = layer_norm(hidden[0].astype(F32), gain_one, shift_one)
    grad_input, grad_gain_one, grad_shift_one = norm_back(
        grad_normed_one, hat_one, inverse_one, gain_one
    )
    grad_input = grad_input + grad_middle

    bias_start = shard_place * head_cols + (ctx_place % groups) * width
    bias_rows = lax.dynamic_update_slice(
        jnp.zeros((2, depth), F32), bias_sums[:2], (0, bias_start)
    )
    vec_terms = jnp.concatenate(
        [
            grad_gain_one[None],
            grad_shift_one[None],
            grad_gain_two[None],
            grad_shift_two[None],
            bias_rows,
            jnp.zeros((2, depth), F32),
        ],
        axis=0,
    )
    vec_sums = butterfly(butterfly(vec_terms, "ctx"), "wsh")
    share_vecs = lax.dynamic_slice_in_dim(vec_sums, ctx_place * own_rows, own_rows, 1).T[:, :6]

    share_qkv, new_qkv, new_first_qkv, new_second_qkv = [
        array.transpose(1, 0, 2)
        for array in adam_parts(
            True,
            share_first,
            *[array.transpose(1, 0, 2) for array in (w_qkv, first_qkv, second_qkv)],
        )
    ]
    share_gu, new_gu, new_first_gu, new_second_gu = adam_parts(
        False, share_gu, w_gu, first_gu, second_gu
    )
    share_down, new_down, new_first_down, new_second_down = [
        array[0]
        for array in adam_parts(True, share_down, w_down[None], first_down[None], second_down[None])
    ]
    share_out, new_out, new_first_out, new_second_out = adam_turned(
        share_first, w_out, first_out, second_out
    )
    new_vecs, new_first_vecs, new_second_vecs = adam_step(
        norm_vecs, share_vecs, first_vecs, second_vecs, 0.0
    )
    return (
        block_out[None],
        grad_input[None],
        share_qkv,
        share_out,
        share_gu,
        share_down,
        share_vecs,
        new_qkv,
        new_out,
        new_gu,
        new_down,
        new_vecs,
        new_first_qkv,
        new_first_out,
        new_first_gu,
        new_first_down,
        new_first_vecs,
        new_second_qkv,
        new_second_out,
        new_second_gu,
        new_second_down,
        new_second_vecs,
    )


def solution(mesh):
    rows = P("wsh", "ctx", None)
    weights = (
        P("ctx", None, "wsh"),
        P("wsh", "ctx"),
        P("ctx", None, "wsh"),
        P("wsh", "ctx"),
        P("ctx", None),
    )
    return jax.shard_map(
        local,
        mesh=mesh,
        in_specs=(rows, rows, P()) + weights * 3,
        out_specs=(rows, rows) + weights * 4,
        check_vma=False,
    )
```

```python
import functools

import jax
import jax.numpy as jnp
from jax import lax
from jax.experimental import pallas as pl
from jax.experimental.pallas import tpu as pltpu
from jax.sharding import PartitionSpec as P


HD = 64
ROT = 16
STEP = 4


learn_rate = 0.005
beta_first = 0.9
beta_second = 0.95
adam_epsilon = 1e-08
weight_decay = 0.1
norm_epsilon = 1e-05
masked_score = -1e30
score_scale = HD ** (-0.5)
F32 = jnp.float32
BF16 = jnp.bfloat16


def swapped(value, axis, bits):
    count = lax.axis_size(axis)
    return lax.ppermute(value, axis, [(source, source ^ bits) for source in range(count)])


def gather_rows(block, axis):
    count = lax.axis_size(axis)
    return [block] + [swapped(block, axis, bits) for bits in range(1, count)]


def scatter_sum(blocks, axis):
    total = blocks[0].astype(F32)
    for bits in range(1, len(blocks)):
        total = total + swapped(blocks[bits], axis, bits).astype(F32)
    return total


def butterfly(value, axis):
    count = lax.axis_size(axis)
    bits = 1
    while bits < count:
        value = value + swapped(value, axis, bits)
        bits *= 2
    return value


def chip_scatter(product, halves, axis):
    count = lax.axis_size("ctx")
    own, other = halves
    sent = product(other).astype(BF16)
    total = (product(own) + swapped(sent, "ctx", 1).astype(F32)).astype(BF16)
    return lax.psum_scatter(
        total,
        "ctx",
        scatter_dimension=axis,
        tiled=True,
        axis_index_groups=[list(range(first, count, 2)) for first in range(2)],
    )


def layer_norm(matrix, gain_vec, shift_vec):
    centre = matrix - jnp.mean(matrix, axis=-1, keepdims=True)
    inverse = lax.rsqrt(jnp.mean(centre * centre, axis=-1, keepdims=True) + norm_epsilon)
    normed = centre * inverse
    return (normed * gain_vec + shift_vec, normed, inverse)


def norm_back(incoming, normed, inverse, gain_vec):
    scaled = incoming * gain_vec
    inner = (
        scaled
        - jnp.mean(scaled, axis=-1, keepdims=True)
        - normed * jnp.mean(scaled * normed, axis=-1, keepdims=True)
    )
    return (inner * inverse, jnp.sum(incoming * normed, axis=0), jnp.sum(incoming, axis=0))


def rotary_tables(positions, width):
    half_rot = ROT // 2
    lane = jnp.arange(width, dtype=jnp.int32) % HD
    frequency = 10000.0 ** (-2.0 * (lane % half_rot).astype(F32) / ROT)
    angles = positions.astype(F32)[:, None] * frequency[None, :]
    turning = (lane < ROT)[None, :]
    low_lane = (lane < half_rot)[None, :]
    cosine = jnp.where(turning, jnp.cos(angles), 1.0)
    sine = jnp.where(turning, jnp.sin(angles), 0.0)
    return cosine, jnp.where(low_lane, -sine, 0.0), jnp.where(low_lane, 0.0, sine)


def turned(value, cosine, from_right, from_left):
    width = value.shape[-1]
    half_rot = ROT // 2
    return (
        value * cosine
        + pltpu.roll(value, width - half_rot, 1) * from_right
        + pltpu.roll(value, half_rot, 1) * from_left
    )


def dot_rows(left_side, right_side):
    return lax.dot_general(
        left_side, right_side, (((0,), (0,)), ((), ())), preferred_element_type=F32
    )


def dot_back(left_side, right_side):
    return lax.dot_general(
        left_side, right_side, (((1,), (1,)), ((), ())), preferred_element_type=F32
    )


def dot(left_side, right_side):
    return jnp.dot(left_side, right_side, preferred_element_type=F32)


def adam_step(master, gradient, first_moment, second_moment, decay_rate):
    moment_one = beta_first * first_moment + (1.0 - beta_first) * gradient
    moment_two = beta_second * second_moment + (1.0 - beta_second) * gradient * gradient
    corrected = moment_one / (1.0 - beta_first**STEP)
    spread = jnp.sqrt(moment_two / (1.0 - beta_second**STEP))
    updated = master - learn_rate * (corrected / (spread + adam_epsilon) + decay_rate * master)
    return (updated, moment_one, moment_two)


def kernel_params(megabytes=48):
    return pltpu.CompilerParams(vmem_limit_bytes=megabytes * 1024 * 1024)


def project_kernel(count, *refs):
    blocks = refs[:count]
    gain, shift, bias_q, bias_v, cosine, from_right, from_left, wq, wk, wv = refs[count : count + 10]
    normed_ref, out_ref = refs[count + 10 :]
    rows, _ = blocks[0].shape
    width = wq.shape[1]

    @pl.when(pl.program_id(0) == 0)
    def _():
        for place in range(count):
            value, _, _ = layer_norm(blocks[place][...].astype(F32), gain[...], shift[...])
            normed_ref[place * rows : (place + 1) * rows, :] = value.astype(BF16)

    for which, weight in enumerate((wq, wk, wv)):
        result = dot(normed_ref[...], weight[...])
        if which == 0:
            result = result + bias_q[...]
        if which == 2:
            result = result + bias_v[...]
        for place in range(count):
            part = result[place * rows : (place + 1) * rows]
            if which < 2:
                part = turned(part, cosine[...], from_right[...], from_left[...])
            out_ref[place, 0, :, which * width : (which + 1) * width] = part.astype(BF16)


def project(blocks, gain, shift, bias_q, bias_v, tables, weights, groups):
    count = len(blocks)
    rows, depth = blocks[0].shape
    head_cols = bias_q.shape[1]
    width = head_cols // groups

    def whole(array):
        return pl.BlockSpec(array.shape, lambda g: (0, 0))

    def column(first):
        return pl.BlockSpec((depth, width), lambda g: (0, first * groups + g))

    operands = [*blocks, gain, shift, bias_q, bias_v, *tables]
    specs = [whole(block) for block in blocks] + [whole(gain), whole(shift)]
    specs += [pl.BlockSpec((1, width), lambda g: (0, g))] * 2
    specs += [whole(table) for table in tables]
    specs += [column(0), column(1), column(2)]
    return pl.pallas_call(
        functools.partial(project_kernel, count),
        grid=(groups,),
        in_specs=specs,
        out_specs=[
            pl.BlockSpec((count * rows, depth), lambda g: (0, 0)),
            pl.BlockSpec((count, 1, rows, 3 * width), lambda g: (0, g, 0, 0)),
        ],
        out_shape=[
            jax.ShapeDtypeStruct((count * rows, depth), BF16),
            jax.ShapeDtypeStruct((count, groups, rows, 3 * width), BF16),
        ],
        compiler_params=kernel_params(),
        cost_estimate=pl.CostEstimate(
            flops=2 * count * rows * depth * 3 * head_cols,
            bytes_accessed=2 * depth * 3 * head_cols + 4 * count * rows * depth,
            transcendentals=0,
        ),
        name="project",
    )(*operands, weights, weights, weights)


def windows(length, most, rows):
    for start in range(0, length, rows):
        first = max(0, (start - (most - 1)) // rows * rows)
        yield start, first, start + rows


def seen(start, first, stop, rows, ids_row, ids_col):
    query_pos = start + lax.broadcasted_iota(jnp.int32, (rows, stop - first), 0)
    key_pos = first + lax.broadcasted_iota(jnp.int32, (rows, stop - first), 1)
    same = ids_row[:, first:stop] == ids_col[start : start + rows, :]
    return (key_pos <= query_pos) & same


def head_mask(width, head):
    lane = lax.broadcasted_iota(jnp.int32, (1, width), 1) // HD
    return jnp.where(lane == head, 1.0, 0.0).astype(F32)


def attend_kernel(count, most, step_rows, me_ref, ids_row_ref, ids_col_ref, *refs):
    pieces = refs[:count]
    att_ref, all_ref, lse_ref = refs[count:]
    rows = pieces[0].shape[0]
    width = pieces[0].shape[1] // 3
    length = count * rows
    me = me_ref[0]
    for bits in range(count):
        place = pl.multiple_of((me ^ bits) * rows, rows)
        all_ref[pl.ds(place, rows), :] = pieces[bits][...]
    ids_row = ids_row_ref[...]
    stat_lane = lax.broadcasted_iota(jnp.int32, (step_rows, 128), 1)
    for start, first, stop in windows(length, most, step_rows):
        allowed = seen(start, first, stop, step_rows, ids_row, ids_col_ref)
        query = all_ref[start : start + step_rows, 0:width]
        key = all_ref[first:stop, width : 2 * width]
        value = all_ref[first:stop, 2 * width : 3 * width]
        stats = jnp.zeros((step_rows, 128), F32)
        total = jnp.zeros((step_rows, width), F32)
        for head in range(width // HD):
            mask = head_mask(width, head).astype(BF16)
            scores = dot_back(query * mask, key) * score_scale
            scores = jnp.where(allowed, scores, masked_score)
            top = jnp.max(scores, axis=-1, keepdims=True)
            weights = jnp.exp(scores - top)
            weight_sum = jnp.sum(weights, axis=-1, keepdims=True)
            total = total + dot(weights.astype(BF16), value * mask) / weight_sum
            stats = jnp.where(stat_lane == head, top + jnp.log(weight_sum), stats)
        att_ref[start : start + step_rows, :] = total.astype(BF16)
        lse_ref[start : start + step_rows, :] = stats


def attend(me, ids_row, ids_col, pieces, most):
    count = len(pieces)
    rows, wide = pieces[0].shape
    width = wide // 3
    length = count * rows
    step_rows = min(256, length)
    vmem = pl.BlockSpec(memory_space=pltpu.VMEM)
    return pl.pallas_call(
        functools.partial(attend_kernel, count, most, step_rows),
        in_specs=[pl.BlockSpec(memory_space=pltpu.SMEM)] + [vmem] * (2 + count),
        out_specs=[vmem] * 3,
        out_shape=[
            jax.ShapeDtypeStruct((length, width), BF16),
            jax.ShapeDtypeStruct((length, wide), BF16),
            jax.ShapeDtypeStruct((length, 128), F32),
        ],
        compiler_params=kernel_params(),
        cost_estimate=pl.CostEstimate(
            flops=4 * length * most * width * 4, bytes_accessed=4 * length * wide, transcendentals=0
        ),
        name="attend",
    )(me, ids_row, ids_col, *pieces)


def attend_back_kernel(
    count, most, step_rows, me_ref, ids_row_ref, ids_col_ref, cos_ref, right_ref, left_ref, *refs
):
    pieces = refs[:count]
    att_ref, all_ref, lse_ref, out_ref, sums_ref, grad_ref, dk_ref, dv_ref = refs[count:]
    rows, width = pieces[0].shape
    length = count * rows
    me = me_ref[0]
    for bits in range(count):
        place = pl.multiple_of((me ^ bits) * rows, rows)
        grad_ref[pl.ds(place, rows), :] = pieces[bits][...]
    dk_ref[...] = jnp.zeros_like(dk_ref)
    dv_ref[...] = jnp.zeros_like(dv_ref)
    ids_row = ids_row_ref[...]
    query_sum = jnp.zeros((1, width), F32)
    for start, first, stop in windows(length, most, step_rows):
        own = slice(start, start + step_rows)
        allowed = seen(start, first, stop, step_rows, ids_row, ids_col_ref)
        query = all_ref[own, 0:width]
        key = all_ref[first:stop, width : 2 * width]
        value = all_ref[first:stop, 2 * width : 3 * width]
        incoming = grad_ref[own, :]
        product = incoming.astype(F32) * att_ref[own, :].astype(F32)
        query_grad = jnp.zeros((step_rows, width), F32)
        key_grad = jnp.zeros((stop - first, width), F32)
        value_grad = jnp.zeros((stop - first, width), F32)
        for head in range(width // HD):
            mask32 = head_mask(width, head)
            mask = mask32.astype(BF16)
            delta = jnp.sum(product * mask32, axis=-1, keepdims=True)
            scores = dot_back(query * mask, key) * score_scale
            probability = jnp.where(
                allowed, jnp.exp(scores - lse_ref[own, head : head + 1]), 0.0
            )
            incoming_head = incoming * mask
            value_grad = value_grad + dot_rows(probability.astype(BF16), incoming_head)
            grad_prob = dot_back(incoming_head, value)
            grad_score = (probability * (grad_prob - delta) * score_scale).astype(BF16)
            query_grad = query_grad + dot(grad_score, key * mask)
            key_grad = key_grad + dot_rows(grad_score, query * mask)
        dk_ref[first:stop, :] += key_grad
        dv_ref[first:stop, :] += value_grad
        query_grad = turned(query_grad, cos_ref[own, :], -right_ref[own, :], -left_ref[own, :])
        query_sum = query_sum + jnp.sum(query_grad, axis=0, keepdims=True)
        out_ref[own, 0:width] = query_grad.astype(BF16)
    out_ref[:, width : 2 * width] = turned(
        dk_ref[...], cos_ref[...], -right_ref[...], -left_ref[...]
    ).astype(BF16)
    value_grad = dv_ref[...]
    out_ref[:, 2 * width : 3 * width] = value_grad.astype(BF16)
    value_sum = jnp.sum(value_grad, axis=0, keepdims=True)
    sums_ref[...] = jnp.concatenate(
        [query_sum, value_sum, jnp.zeros((6, width), F32)], axis=0
    )


def attend_back(me, ids_row, ids_col, tables, pieces, att, everything, lse, most):
    count = len(pieces)
    rows, width = pieces[0].shape
    length = count * rows
    step_rows = min(256, length)
    vmem = pl.BlockSpec(memory_space=pltpu.VMEM)
    return pl.pallas_call(
        functools.partial(attend_back_kernel, count, most, step_rows),
        in_specs=[pl.BlockSpec(memory_space=pltpu.SMEM)] + [vmem] * (8 + count),
        out_specs=[vmem] * 2,
        out_shape=[
            jax.ShapeDtypeStruct((length, 3 * width), BF16),
            jax.ShapeDtypeStruct((8, width), F32),
        ],
        scratch_shapes=[
            pltpu.VMEM((length, width), BF16),
            pltpu.VMEM((length, width), F32),
            pltpu.VMEM((length, width), F32),
        ],
        compiler_params=kernel_params(),
        cost_estimate=pl.CostEstimate(
            flops=10 * length * most * width * 4,
            bytes_accessed=16 * length * width,
            transcendentals=0,
        ),
        name="attend_back",
    )(me, ids_row, ids_col, *tables, *pieces, att, everything, lse)


def halve_kernel(chips, me_ref, matrix_ref, own_ref, other_ref):
    core = me_ref[0] % 2
    cols = matrix_ref.shape[1] // (2 * chips)
    for chip in range(chips):
        into = slice(chip * cols, (chip + 1) * cols)
        for out_ref, which in ((own_ref, core), (other_ref, 1 - core)):
            start = pl.multiple_of((2 * chip + which) * cols, cols)
            out_ref[:, into] = matrix_ref[:, pl.ds(start, cols)]


def halve(me, matrix, chips):
    rows, cols = matrix.shape
    vmem = pl.BlockSpec(memory_space=pltpu.VMEM)
    return pl.pallas_call(
        functools.partial(halve_kernel, chips),
        in_specs=[pl.BlockSpec(memory_space=pltpu.SMEM), vmem],
        out_specs=[vmem] * 2,
        out_shape=[jax.ShapeDtypeStruct((rows, cols // 2), BF16)] * 2,
        compiler_params=kernel_params(),
        cost_estimate=pl.CostEstimate(
            flops=0, bytes_accessed=4 * rows * cols, transcendentals=0
        ),
        name="halve",
    )(me, matrix)


def pack_kernel(qkv_ref, out_ref, packed_ref):
    head_cols = qkv_ref.shape[2]
    for which in range(3):
        packed_ref[:, which * head_cols : (which + 1) * head_cols] = qkv_ref[which].astype(BF16)
    packed_ref[:, 3 * head_cols : 4 * head_cols] = out_ref[...].T.astype(BF16)


def pack(w_qkv, w_out):
    _, rows, head_cols = w_qkv.shape
    vmem = pl.BlockSpec(memory_space=pltpu.VMEM)
    return pl.pallas_call(
        pack_kernel,
        in_specs=[vmem] * 2,
        out_specs=vmem,
        out_shape=jax.ShapeDtypeStruct((rows, 4 * head_cols), BF16),
        compiler_params=kernel_params(),
        name="pack",
    )(w_qkv, w_out)


def adam_kernel(leading, share_ref, master_ref, first_ref, second_ref, *outs):
    parts = master_ref.shape[0 if leading else 1]
    cols = master_ref.shape[2]
    for part in range(parts):
        spot = (part,) if leading else (slice(None), part)
        gradient = share_ref[:, part * cols : (part + 1) * cols].astype(F32)
        updates = adam_step(
            master_ref[spot], gradient, first_ref[spot], second_ref[spot], weight_decay
        )
        for out_ref, value in zip(outs, (gradient, *updates)):
            out_ref[spot] = value


def adam_parts(leading, share, *arrays):
    shape = arrays[0].shape
    rows, width = share.shape
    step_rows = max(
        size
        for size in range(16, rows + 1, 16)
        if rows % size == 0 and (size == 16 or size * width <= 100000)
    )
    if leading:
        block = pl.BlockSpec((shape[0], step_rows, shape[2]), lambda step: (0, step, 0))
    else:
        block = pl.BlockSpec((step_rows, shape[1], shape[2]), lambda step: (step, 0, 0))
    return pl.pallas_call(
        functools.partial(adam_kernel, leading),
        grid=(rows // step_rows,),
        in_specs=[pl.BlockSpec((step_rows, width), lambda step: (step, 0))] + [block] * 3,
        out_specs=[block] * 4,
        out_shape=[jax.ShapeDtypeStruct(shape, F32)] * 4,
        compiler_params=kernel_params(),
        cost_estimate=pl.CostEstimate(
            flops=0, bytes_accessed=30 * rows * width, transcendentals=0
        ),
        name="adam",
    )(share, *arrays)


def place_kernel(count, groups, parts, me_ref, *refs):
    pieces = refs[:count]
    out_ref = refs[count]
    rows = pieces[0].shape[0]
    width = pieces[0].shape[1] // parts
    for bits in range(count):
        source = me_ref[0] ^ bits
        row = pl.multiple_of(((source // groups) ^ me_ref[1]) * rows, rows)
        for part in range(parts):
            col = pl.multiple_of((part * groups + source % groups) * width, width)
            out_ref[pl.ds(row, rows), pl.ds(col, width)] = pieces[bits][
                :, part * width : (part + 1) * width
            ]


def place(places, pieces, groups, parts):
    count = len(pieces)
    rows, wide = pieces[0].shape
    vmem = pl.BlockSpec(memory_space=pltpu.VMEM)
    return pl.pallas_call(
        functools.partial(place_kernel, count, groups, parts),
        in_specs=[pl.BlockSpec(memory_space=pltpu.SMEM)] + [vmem] * count,
        out_specs=vmem,
        out_shape=jax.ShapeDtypeStruct((count // groups * rows, groups * wide), BF16),
        compiler_params=kernel_params(),
        cost_estimate=pl.CostEstimate(
            flops=0, bytes_accessed=4 * count * rows * wide, transcendentals=0
        ),
        name="place",
    )(places, *pieces)


def local(
    hidden,
    cotangent,
    doc_ids,
    w_qkv,
    w_out,
    w_gu,
    w_down,
    norm_vecs,
    first_qkv,
    first_out,
    first_gu,
    first_down,
    first_vecs,
    second_qkv,
    second_out,
    second_gu,
    second_down,
    second_vecs,
):
    ctx_size = lax.axis_size("ctx")
    ctx_place = lax.axis_index("ctx")
    shard_count = lax.axis_size("wsh")
    shard_place = lax.axis_index("wsh")
    tok_rows = hidden.shape[1]
    depth = hidden.shape[2]
    length = doc_ids.shape[1]
    most = length // 2
    head_cols = w_qkv.shape[2]
    unit_cols = w_gu.shape[2]
    own_rows = w_qkv.shape[0]
    groups = ctx_size // shard_count
    width = head_cols // groups
    ctx_scalar = ctx_place.astype(jnp.int32).reshape(1)
    places = jnp.stack([ctx_place, shard_place]).astype(jnp.int32)

    first_weights = pack(w_qkv.transpose(1, 0, 2), w_out)
    first_all = lax.all_gather(first_weights, "ctx", axis=0, tiled=True)
    gu_part = w_gu.astype(BF16).reshape(own_rows, 2 * unit_cols)
    gu_flat = lax.all_gather(gu_part, "ctx", axis=0, tiled=True)
    down_weight = lax.all_gather(w_down.astype(BF16), "ctx", axis=1, tiled=True)

    hidden_blocks = gather_rows(hidden[0], "wsh")
    cot_all = jnp.concatenate(gather_rows(cotangent[0], "wsh"), axis=0)

    own_seq = ctx_place // groups
    ids_own = lax.dynamic_slice_in_dim(doc_ids, own_seq, 1, 0)
    ids_col = ids_own.reshape(length, 1)
    positions = ctx_place * tok_rows + jnp.arange(tok_rows, dtype=jnp.int32)
    tables = rotary_tables(positions, width)
    tables_all = rotary_tables(jnp.arange(length, dtype=jnp.int32), width)

    own_vectors = jnp.pad(norm_vecs.astype(BF16).astype(F32).T, ((0, 2), (0, 0)))
    vectors = butterfly(
        lax.dynamic_update_slice(
            jnp.zeros((8, depth), F32), own_vectors, (0, ctx_place * own_rows)
        ),
        "ctx",
    )
    gain_one, shift_one, gain_two, shift_two = [vectors[row : row + 1] for row in range(4)]
    col_start = shard_place * head_cols
    bias_query = lax.dynamic_slice_in_dim(vectors[4:5], col_start, head_cols, 1)
    bias_value = lax.dynamic_slice_in_dim(vectors[5:6], col_start, head_cols, 1)
    qkv_flat = first_all[:, : 3 * head_cols]
    out_turned = first_all[:, 3 * head_cols :]

    gathered_one, projected = project(
        hidden_blocks, gain_one, shift_one, bias_query, bias_value, tables, first_all, groups
    )

    def exchange_out(array, bits):
        target = ctx_place ^ bits
        picked = lax.dynamic_slice(
            array,
            ((target // groups) ^ shard_place, target % groups, 0, 0),
            (1, 1) + array.shape[2:],
        )[0, 0]
        return picked if bits == 0 else swapped(picked, "ctx", bits)

    def exchange_back(array, bits):
        picked = lax.dynamic_slice_in_dim(array, (ctx_place ^ bits) * tok_rows, tok_rows, 0)
        return picked if bits == 0 else swapped(picked, "ctx", bits)

    pieces = [exchange_out(projected, bits) for bits in range(ctx_size)]
    att_own, qkv_own, log_sums = attend(ctx_scalar, ids_own, ids_col, pieces, most)
    attended = place(
        places, [exchange_back(att_own, bits) for bits in range(ctx_size)], groups, 1
    )

    def row_blocks(matrix):
        return [
            matrix[place_row * tok_rows : (place_row + 1) * tok_rows]
            for place_row in range(shard_count)
        ]

    attn_terms = dot_back(attended, out_turned).astype(BF16)
    middle = hidden[0].astype(F32) + scatter_sum(row_blocks(attn_terms), "wsh")
    normed_two, hat_two, inverse_two = layer_norm(middle, gain_two, shift_two)
    gathered_two = jnp.concatenate(gather_rows(normed_two.astype(BF16), "wsh"), axis=0)
    gate_up = dot(gathered_two, gu_flat)
    gate_part = gate_up[:, :unit_cols]
    activated = (gate_part * jax.nn.sigmoid(gate_part) * gate_up[:, unit_cols:]).astype(BF16)
    share_down = chip_scatter(lambda half: dot_rows(activated, half), halve(ctx_scalar, cot_all, ctx_size // 2), 1)

    gate_up = lax.optimization_barrier(gate_up)
    gate_part = gate_up[:, :unit_cols]
    up_part = gate_up[:, unit_cols:]
    sigmoid_gate = jax.nn.sigmoid(gate_part)
    grad_act = dot_back(cot_all, down_weight)
    grad_gate = grad_act * up_part * sigmoid_gate * (1.0 + gate_part * (1.0 - sigmoid_gate))
    grad_up = grad_act * gate_part * sigmoid_gate
    grad_gate_up = jnp.concatenate([grad_gate, grad_up], axis=1).astype(BF16)
    share_gu = chip_scatter(lambda half: dot_rows(half, grad_gate_up), halve(ctx_scalar, gathered_two, ctx_size // 2), 0)
    normed_two_terms = dot_back(grad_gate_up, gu_flat).astype(BF16)
    grad_normed_two = scatter_sum(row_blocks(normed_two_terms), "wsh")
    grad_middle, grad_gain_two, grad_shift_two = norm_back(
        grad_normed_two, hat_two, inverse_two, gain_two
    )
    grad_middle = grad_middle + cotangent[0].astype(F32)
    middle_all = jnp.concatenate(gather_rows(grad_middle.astype(BF16), "wsh"), axis=0)
    share_out = chip_scatter(lambda half: dot_rows(attended, half), halve(ctx_scalar, middle_all, ctx_size // 2), 1)
    grad_att = dot(middle_all, out_turned).astype(BF16)

    def exchange_grad(bits):
        target = ctx_place ^ bits
        row = ((target // groups) ^ shard_place) * tok_rows
        picked = lax.dynamic_slice(
            grad_att, (row, target % groups * width), (tok_rows, width)
        )
        return picked if bits == 0 else swapped(picked, "ctx", bits)

    grad_pieces = [exchange_grad(bits) for bits in range(ctx_size)]
    grad_own, bias_sums = attend_back(
        ctx_scalar, ids_own, ids_col, tables_all, grad_pieces, att_own, qkv_own, log_sums, most
    )
    grad_rows = place(
        places, [exchange_back(grad_own, bits) for bits in range(ctx_size)], groups, 3
    )
    share_qkv = chip_scatter(lambda half: dot_rows(half, grad_rows), halve(ctx_scalar, gathered_one, ctx_size // 2), 0)

    late_activated, late_middle, _ = lax.optimization_barrier((activated, middle, grad_rows))
    ffn_terms = dot(late_activated, down_weight).astype(BF16)
    ffn_sum = scatter_sum(row_blocks(ffn_terms), "wsh")
    block_out = (late_middle + ffn_sum).astype(BF16)

    normed_one_terms = dot_back(grad_rows, qkv_flat).astype(BF16)
    grad_normed_one = scatter_sum(row_blocks(normed_one_terms), "wsh")
    _, hat_one, inverse_one = layer_norm(hidden[0].astype(F32), gain_one, shift_one)
    grad_input, grad_gain_one, grad_shift_one = norm_back(
        grad_normed_one, hat_one, inverse_one, gain_one
    )
    grad_input = grad_input + grad_middle

    bias_start = shard_place * head_cols + (ctx_place % groups) * width
    bias_rows = lax.dynamic_update_slice(
        jnp.zeros((2, depth), F32), bias_sums[:2], (0, bias_start)
    )
    vec_terms = jnp.concatenate(
        [
            grad_gain_one[None],
            grad_shift_one[None],
            grad_gain_two[None],
            grad_shift_two[None],
            bias_rows,
            jnp.zeros((2, depth), F32),
        ],
        axis=0,
    )
    vec_share = scatter_sum(
        [
            lax.dynamic_slice_in_dim(vec_terms, (ctx_place ^ bits) * own_rows, own_rows, 1)
            for bits in range(ctx_size)
        ],
        "ctx",
    )
    vec_share = scatter_sum([vec_share] * shard_count, "wsh")
    share_vecs = vec_share.T[:, :6]

    share_qkv, new_qkv, new_first_qkv, new_second_qkv = [
        array.transpose(1, 0, 2)
        for array in adam_parts(
            True,
            share_qkv,
            *[array.transpose(1, 0, 2) for array in (w_qkv, first_qkv, second_qkv)],
        )
    ]
    share_gu, new_gu, new_first_gu, new_second_gu = adam_parts(
        False, share_gu, w_gu, first_gu, second_gu
    )
    share_down, new_down, new_first_down, new_second_down = [
        array[0]
        for array in adam_parts(True, share_down, w_down[None], first_down[None], second_down[None])
    ]
    share_out, new_out, new_first_out, new_second_out = [
        array[0]
        for array in adam_parts(
            True, share_out, w_out[None], first_out[None], second_out[None]
        )
    ]
    new_vecs, new_first_vecs, new_second_vecs = adam_step(
        norm_vecs, share_vecs, first_vecs, second_vecs, 0.0
    )
    return (
        block_out[None],
        grad_input[None],
        share_qkv,
        share_out,
        share_gu,
        share_down,
        share_vecs,
        new_qkv,
        new_out,
        new_gu,
        new_down,
        new_vecs,
        new_first_qkv,
        new_first_out,
        new_first_gu,
        new_first_down,
        new_first_vecs,
        new_second_qkv,
        new_second_out,
        new_second_gu,
        new_second_down,
        new_second_vecs,
    )


def solution(mesh):
    rows = P("wsh", "ctx", None)
    weights = (
        P("ctx", None, "wsh"),
        P("wsh", "ctx"),
        P("ctx", None, "wsh"),
        P("wsh", "ctx"),
        P("ctx", None),
    )
    return jax.shard_map(
        local,
        mesh=mesh,
        in_specs=(rows, rows, P()) + weights * 3,
        out_specs=(rows, rows) + weights * 4,
        check_vma=False,
    )
```
